512 devices in a mesh: shot: 16 (over x, z_lo), blk: 32 (over z_hi, y, core).
Axes of the slice: x: 4, y: 8, z: 8 (z_hi: 2, z_lo: 4; z = z_hi * 4 + z_lo), core: 2. Of those that a mesh axis runs over, the one named last changes fastest.
Arguments:
- state_before: float32 [16, 256, 64, 128], P('shot', 'blk'), may hold values from -7 to 7
- state_now: float32 [16, 256, 64, 128], P('shot', 'blk'), may hold values from -7 to 7
- adjoint_later: float32 [16, 256, 64, 128], P('shot', 'blk'), may hold values from -7 to 7
- adjoint_now: float32 [16, 256, 64, 128], P('shot', 'blk'), may hold values from -7 to 7
- courant_sq: float32 [256, 128, 128], P('blk', 'shot'), may hold values from 0.02 to 0.3
- epsilon: float32 [256, 128, 128], P('blk', 'shot'), may hold values from 0.02 to 0.3
- tilt_angle: float32 [256, 128, 128], P('blk', 'shot'), may hold values from 0 to 1.2
- azimuth: float32 [256, 128, 128], P('blk', 'shot'), may hold values from -3.140625 to 3.140625
- aperture_anchor: int32 [16], P('shot'), may hold values from 0 to 64, as said below
- step_index: int32 [1], replicated, may hold values from 0 to 12
- wavelet: float32 [16, 16], P('shot'), may hold values from -8 to 8
- residual_traces: float32 [16, 16, 128], P('shot'), may hold values from -6 to 6
- source_x: int32 [16], P('shot'), may hold values from 0 to 255
- source_y: int32 [16], P('shot'), may hold values from 0 to 63
- source_z: int32 [16], P('shot'), may hold values from 0 to 127
- receiver_x: int32 [16, 128], P('shot'), may hold values from 0 to 255
- receiver_y: int32 [16, 128], P('shot'), may hold values from 0 to 63
- receiver_z: int32 [16, 128], P('shot'), may hold values from 0 to 127
Outputs:
- adjoint_one: float32 [16, 256, 64, 128], P('shot', 'blk')
- adjoint_zero: float32 [16, 256, 64, 128], P('shot', 'blk')
- model_grad: float32 [256, 128, 128], P('blk', 'shot')
The draws below stay inside these ranges and needn't reach their ends.
Inputs may be any that keep to these rules, and one draw needn't show every extreme that they name: `aperture_anchor`: each value is a multiple of 8; some shot has 0 and some shot has 64.
All inputs are finite; a program needn't handle non-finite values.
Results may differ from the reference program's by a relative error of at most 0.0003.
Values sent between devices are 32-bit elements; how exact they have to be, the bound alone decides.
A program may use at most 64 MiB of HBM per device.

```python
import jax
import jax.numpy as jnp
from jax import lax

NY = 64
NZ = 128
STEPS = 4
NT = 16
NREC = 128
SHOTS = 16
AX = 256
NYG = 128
YSH = 8


def draw_aperture_anchor(key, part):
    positions = (NYG - NY) // YSH + 1
    picked = jax.random.randint(key, (SHOTS,), 0, positions)
    ordering = jax.random.permutation(jax.random.fold_in(key, 7), SHOTS)
    picked = jnp.where(ordering == 0, 0, jnp.where(ordering == 1, positions - 1, picked))
    return (picked * YSH).astype(jnp.int32)


def state_field(key, salt):
    folded = jax.random.fold_in(key, salt)
    random_part = jnp.clip(jax.random.normal(folded, (SHOTS, AX, NY, NZ), jnp.float32), -6.0, 6.0)
    return random_part.astype(jnp.float32)


def draw_state_before(key, part):
    return state_field(key, 101)


def draw_state_now(key, part):
    return state_field(key, 202)


def draw_adjoint_later(key, part):
    return state_field(key, 303)


def draw_adjoint_now(key, part):
    return state_field(key, 404)


def place_ends(values, own_key, low, top_value):
    index_at = [jax.random.randint(jax.random.fold_in(own_key, axis), (), 0, length) for axis, length in enumerate(values.shape)]
    widest = values.shape.index(max(values.shape))
    next_to = index_at[:widest] + [(index_at[widest] + 1) % values.shape[widest]] + index_at[widest + 1:]
    return values.at[tuple(index_at)].set(low).at[tuple(next_to)].set(top_value)


def levels(key, shape, pieces, low, high):
    def one(position, shards_of):
        draws = jax.random.uniform(jax.random.fold_in(jax.random.fold_in(key, 6), position), (shards_of,), jnp.float32, low / len(pieces), high / len(pieces))
        return jnp.repeat(jnp.exp(draws), shape[position] // shards_of).reshape((-1,) + (1,) * (len(shape) - position - 1))

    level = one(*pieces[0])
    for cut in pieces[1:]:
        level = level * one(*cut)
    return level


def centred(stream_key, shape, width, bound, split=(), held_as=jnp.bfloat16):
    array = width * jax.random.normal(stream_key, shape, jnp.float32)
    if split:
        array = array * levels(stream_key, shape, split, -0.22, 0.18)
    return jnp.clip(array, -bound, bound).astype(held_as)


def setup_inputs(seed: int = 0) -> dict:
    key_of = jax.random.split(jax.random.key(seed), 19)
    state_before = draw_state_before(jax.random.fold_in(key_of[18], 71), 0)
    state_now = draw_state_now(jax.random.fold_in(key_of[18], 71), 0)
    adjoint_later = draw_adjoint_later(jax.random.fold_in(key_of[18], 71), 0)
    adjoint_now = draw_adjoint_now(jax.random.fold_in(key_of[18], 71), 0)
    courant_sq = jnp.clip(0.02 + 0.28 * jax.random.uniform(key_of[4], (AX, NYG, NZ), jnp.float32) ** levels(key_of[4], (AX, NYG, NZ), ((0, 32), (1, 16)), -0.2, 0.2), 0.02, 0.3)
    epsilon = jnp.clip(0.02 + 0.28 * jax.random.uniform(key_of[5], (AX, NYG, NZ), jnp.float32) ** levels(key_of[5], (AX, NYG, NZ), ((0, 32), (1, 16)), -0.2, 0.2), 0.02, 0.3)
    tilt_angle = jnp.clip(1.2 * jax.random.uniform(key_of[6], (AX, NYG, NZ), jnp.float32) ** levels(key_of[6], (AX, NYG, NZ), ((0, 32), (1, 16)), -0.2, 0.2), 0.0, 1.2)
    azimuth = jnp.clip(jax.random.uniform(key_of[7], (AX, NYG, NZ), jnp.float32, -3.140625, 3.140625), -3.140625, 3.140625)
    aperture_anchor = draw_aperture_anchor(jax.random.fold_in(key_of[18], 71), 0)
    step_index = jax.random.randint(key_of[9], (1,), 0, NT - STEPS + 1).astype(jnp.int32)
    wavelet = centred(key_of[10], (SHOTS, NT), 2.0, 8.0, ((0, 16),), jnp.float32)
    residual_traces = centred(key_of[11], (SHOTS, NT, NREC), 1.0, 6.0, ((0, 16),), jnp.float32)
    source_x = place_ends(jax.random.randint(key_of[12], (SHOTS,), 0, AX), jax.random.fold_in(key_of[12], 1), 0, AX - 1).astype(jnp.int32)
    source_y = place_ends(jax.random.randint(key_of[13], (SHOTS,), 0, NY), jax.random.fold_in(key_of[13], 1), 0, NY - 1).astype(jnp.int32)
    source_z = place_ends(jax.random.randint(key_of[14], (SHOTS,), 0, NZ), jax.random.fold_in(key_of[14], 1), 0, NZ - 1).astype(jnp.int32)
    receiver_x = place_ends(jax.random.randint(key_of[15], (SHOTS, NREC), 0, AX), jax.random.fold_in(key_of[15], 1), 0, AX - 1).astype(jnp.int32)
    receiver_y = place_ends(jax.random.randint(key_of[16], (SHOTS, NREC), 0, NY), jax.random.fold_in(key_of[16], 1), 0, NY - 1).astype(jnp.int32)
    receiver_z = place_ends(jax.random.randint(key_of[17], (SHOTS, NREC), 0, NZ), jax.random.fold_in(key_of[17], 1), 0, NZ - 1).astype(jnp.int32)
    return {"state_before": state_before, "state_now": state_now, "adjoint_later": adjoint_later, "adjoint_now": adjoint_now, "courant_sq": courant_sq, "epsilon": epsilon, "tilt_angle": tilt_angle, "azimuth": azimuth, "aperture_anchor": aperture_anchor, "step_index": step_index, "wavelet": wavelet, "residual_traces": residual_traces, "source_x": source_x, "source_y": source_y, "source_z": source_z, "receiver_x": receiver_x, "receiver_y": receiver_y, "receiver_z": receiver_z}


COEF = (0.8, -0.2, 4.0 / 105.0, -1.0 / 280.0)


def first_diff(padded, axis, count):
    summed = None
    for k in range(1, 5):
        upper_part = lax.slice_in_dim(padded, 4 + k, 4 + k + count, axis=axis)
        lower_part = lax.slice_in_dim(padded, 4 - k, 4 - k + count, axis=axis)
        addend = COEF[k - 1] * (upper_part - lower_part)
        summed = addend if summed is None else summed + addend
    return summed


def pad_axis(field, axis):
    widths = [(0, 0), (0, 0), (0, 0)]
    widths[axis] = (4, 4)
    return jnp.pad(field, widths)


def operate(field, tensor_parts):
    twice_eps, normal_x, normal_y, normal_z = tensor_parts
    slope_x = first_diff(pad_axis(field, 0), 0, field.shape[0])
    slope_y = first_diff(pad_axis(field, 1), 1, field.shape[1])
    slope_z = first_diff(pad_axis(field, 2), 2, field.shape[2])
    normal_slope = normal_x * slope_x + normal_y * slope_y + normal_z * slope_z
    flux_x = (1.0 + twice_eps) * slope_x - twice_eps * normal_x * normal_slope
    flux_y = (1.0 + twice_eps) * slope_y - twice_eps * normal_y * normal_slope
    flux_z = (1.0 + twice_eps) * slope_z - twice_eps * normal_z * normal_slope
    result = first_diff(pad_axis(flux_x, 0), 0, field.shape[0])
    result = result + first_diff(pad_axis(flux_y, 1), 1, field.shape[1])
    return result + first_diff(pad_axis(flux_z, 2), 2, field.shape[2])


def reference(state_before, state_now, adjoint_later, adjoint_now, courant_sq, epsilon, tilt_angle, azimuth, aperture_anchor, step_index, wavelet, residual_traces, source_x, source_y, source_z, receiver_x, receiver_y, receiver_z):
    start_step = step_index[0].astype(jnp.int32)

    def one_shot(grad_whole, shot_index):
        anchor = aperture_anchor[shot_index].astype(jnp.int32)

        def window(field):
            return lax.dynamic_slice_in_dim(field, anchor, NY, axis=1)

        speed_term = window(courant_sq)
        twice_eps = 2.0 * window(epsilon)
        tilt_part = window(tilt_angle)
        azimuth_part = window(azimuth)
        tensor_parts = (twice_eps, jnp.sin(tilt_part) * jnp.cos(azimuth_part), jnp.sin(tilt_part) * jnp.sin(azimuth_part), jnp.cos(tilt_part))
        previous = state_before[shot_index]
        current = state_now[shot_index]
        images = []
        for t in range(STEPS):
            image = operate(current, tensor_parts)
            images.append(image)
            if t < STEPS - 1:
                amplitude = lax.dynamic_index_in_dim(wavelet[shot_index], (start_step + t).astype(jnp.int32), keepdims=False)
                following = 2.0 * current - previous + speed_term * image
                following = following.at[source_x[shot_index], source_y[shot_index], source_z[shot_index]].add(amplitude)
                previous, current = current, following
        later = adjoint_later[shot_index]
        present = adjoint_now[shot_index]
        shot_grad = jnp.zeros((AX, NY, NZ), jnp.float32)
        for t in reversed(range(STEPS)):
            shot_grad = shot_grad + present * images[t]
            earlier = 2.0 * present - later + operate(speed_term * present, tensor_parts)
            samples = lax.dynamic_index_in_dim(residual_traces[shot_index], (start_step + t).astype(jnp.int32), keepdims=False)
            earlier = earlier.at[receiver_x[shot_index], receiver_y[shot_index], receiver_z[shot_index]].add(samples)
            later, present = present, earlier
        placed = lax.dynamic_slice_in_dim(grad_whole, anchor, NY, axis=1) + shot_grad
        zero_index = jnp.zeros((), jnp.int32)
        grad_whole = lax.dynamic_update_slice(grad_whole, placed, (zero_index, anchor, zero_index))
        return grad_whole, (later, present)

    grad_start = jnp.zeros((AX, NYG, NZ), jnp.float32)
    grad_whole, (adjoint_one, adjoint_zero) = lax.scan(one_shot, grad_start, jnp.arange(SHOTS, dtype=jnp.int32))
    return (adjoint_one, adjoint_zero, grad_whole)
```

```python
import functools
import math

import numpy as np
import jax
import jax.numpy as jnp
from jax import lax
from jax.experimental import pallas as pl
from jax.experimental.pallas import tpu as pltpu
from jax.sharding import PartitionSpec as P

STEPS = 4
COEF = (0.8, -0.2, 4.0 / 105.0, -1.0 / 280.0)
WHOLE = (672, -168, 32, -3)
MESH = pl.DeviceIdType.MESH
F32 = jnp.float32

X, Y, Z = 8, 64, 128
PAD = 8
PLACES = 9
NX, NZL = 4, 4


def depth_matrix():
    m = np.zeros((Z, Z), np.float32)
    for k in range(1, 5):
        for j in range(Z):
            if j + k < Z:
                m[j + k, j] += WHOLE[k - 1]
            if j - k >= 0:
                m[j - k, j] -= WHOLE[k - 1]
    return jnp.asarray(np.concatenate([m, m], 0), jnp.bfloat16)


def sin_cos(angle):
    square = angle * angle
    sine = jnp.full_like(angle, 1.0 / math.factorial(13))
    for n in (11, 9, 7, 5, 3, 1):
        sine = sine * square + (-1.0) ** (n // 2) / math.factorial(n)
    cosine = jnp.full_like(angle, -1.0 / math.factorial(14))
    for n in (12, 10, 8, 6, 4, 2, 0):
        cosine = cosine * square + (-1.0) ** (n // 2) / math.factorial(n)
    return sine * angle, cosine


def depth_diff(flat, matrix):
    upper = flat.astype(jnp.bfloat16)
    lower = (flat - upper.astype(F32)).astype(jnp.bfloat16)
    both = jnp.concatenate([upper, lower], axis=1)
    return jnp.dot(both, matrix, preferred_element_type=F32) * (1.0 / 840.0)


def kernel(
    blocks,
    pick_ref, amp_ref,
    before_ref, now_ref, later_ref, adj_ref,
    c_ref, eps_ref, tilt_ref, az_ref, inj_ref, at_ref, mat_ref,
    one_ref, zero_ref, grad_ref,
    g_ref, m_ref, u_ref, v_ref, old_ref, lam_ref, img_ref, cw_ref,
    e1_ref, e_ref, nx_ref, ny_ref, nz_ref,
    slz_ref, fx_ref, fy_ref, fz_ref,
    gp_ref, xs_ref, xr_ref, sum_ref, zr_ref,
    zs_sem, zr_sem, xs_sem, xr_sem, hs_sem, hr_sem, ms_sem, mr_sem,
    fs_sem, fr_sem, rs_sem, rr_sem, qs_sem, qr_sem,
):
    shot = lax.axis_index("shot")
    blk = lax.axis_index("blk")
    px = shot // NZL
    pz = shot % NZL
    has_left = blk > 0
    has_right = blk < blocks - 1
    shots_z = [px * NZL + (pz + k) % NZL for k in range(1, NZL)]
    shots_x = [((px + k) % NX) * NZL + pz for k in range(1, NX)]

    barrier = pltpu.get_barrier_semaphore()
    for other in shots_z + shots_x:
        pl.semaphore_signal(barrier, inc=1, device_id=(other, blk), device_id_type=MESH)

    @pl.when(has_left)
    def _():
        pl.semaphore_signal(barrier, inc=1, device_id=(shot, blk - 1), device_id_type=MESH)

    @pl.when(has_right)
    def _():
        pl.semaphore_signal(barrier, inc=1, device_id=(shot, blk + 1), device_id_type=MESH)

    peers = len(shots_z) + len(shots_x)

    @pl.when(has_left & has_right)
    def _():
        pl.semaphore_wait(barrier, peers + 2)

    @pl.when(jnp.logical_not(has_left & has_right))
    def _():
        pl.semaphore_wait(barrier, peers + 1)

    def remote(src, dst, ssem, rsem, device):
        return pltpu.make_async_remote_copy(
            src_ref=src, dst_ref=dst, send_sem=ssem, recv_sem=rsem,
            device_id=device, device_id_type=MESH,
        )

    class Pair:
        def __init__(self, src_right, dst_left_halo, src_left, dst_right_halo, ssem, rsem):
            self.right = remote(src_right, dst_left_halo, ssem.at[0], rsem.at[0], (shot, blk + 1))
            self.left = remote(src_left, dst_right_halo, ssem.at[1], rsem.at[1], (shot, blk - 1))

        def start(self):
            @pl.when(has_right)
            def _():
                self.right.start()

            @pl.when(has_left)
            def _():
                self.left.start()

        def wait_recv(self):
            @pl.when(has_left)
            def _():
                self.right.wait_recv()

            @pl.when(has_right)
            def _():
                self.left.wait_recv()

        def wait_send(self):
            @pl.when(has_right)
            def _():
                self.right.wait_send()

            @pl.when(has_left)
            def _():
                self.left.wait_send()

    def field_pair(ref, chain, p, src=None):
        own = ref.at[p, X:2 * X, PAD:PAD + Y] if src is None else src
        return Pair(
            own, ref.at[p, 0:X, PAD:PAD + Y], own, ref.at[p, 2 * X:3 * X, PAD:PAD + Y],
            fs_sem.at[chain, p], fr_sem.at[chain, p],
        )

    first_forward = field_pair(u_ref, 0, 0, now_ref.at[0])
    first_forward.start()

    models = (c_ref, eps_ref, tilt_ref, az_ref)
    fields = len(models)

    def z_copy(i, k):
        rows = pl.ds(pl.multiple_of(shot * 8, 8), 8)
        return remote(models[i], g_ref.at[i, :, rows], zs_sem.at[i, k - 1], zr_sem.at[i, k - 1], (shots_z[k - 1], blk))

    def x_copy(i, side):
        rows = pl.ds(pl.multiple_of(px * 32, 8), 32)
        part = g_ref.at[i, :, rows]
        return remote(part, part, xs_sem.at[i, side], xr_sem.at[i, side], (shots_x[0 if side == 0 else 2], blk))

    def x_forward(i, side):
        origin = (px + (3 if side == 0 else 1)) % NX
        rows = pl.ds(pl.multiple_of(origin * 32 + 16 * side, 8), 16)
        part = g_ref.at[i, :, rows]
        return remote(part, part, hs_sem.at[i, side], hr_sem.at[i, side], (shots_x[0 if side == 0 else 2], blk))

    for i in range(fields):
        for k in range(1, NZL):
            z_copy(i, k).start()

    own_rows = pl.ds(pl.multiple_of(shot * 8, 8), 8)
    for i in range(fields):
        g_ref[i, :, own_rows, :] = models[i][...]
    zeros_y = jnp.zeros((3 * X, PAD, Z), F32)
    for p in range(2):
        for ref in (u_ref, v_ref):
            ref[p, :, 0:PAD, :] = zeros_y
            ref[p, :, PAD + Y:, :] = zeros_y
    fy_ref[:, 0:PAD, :] = jnp.zeros((X, PAD, Z), F32)
    fy_ref[:, PAD + Y:, :] = jnp.zeros((X, PAD, Z), F32)

    def edge(at, m_at):
        def row(j, carry):
            for p in range(2):
                for ref in (u_ref, v_ref):
                    ref[p, at + j, PAD:PAD + Y, :] = jnp.zeros((Y, Z), F32)
            return carry

        lax.fori_loop(0, X, row, 0)

        def m_row(j, carry):
            for i in range(3):
                m_ref[i, m_at + j] = jnp.zeros((Y, Z), F32)
            return carry

        lax.fori_loop(0, 4, m_row, 0)

    @pl.when(blk == 0)
    def _():
        edge(0, 0)

    @pl.when(blk == blocks - 1)
    def _():
        edge(2 * X, 12)


    def setup_row(j, carry):
        u_ref[0, X + j, PAD:PAD + Y, :] = now_ref[0, j]
        old_ref[0, j] = before_ref[0, j]
        old_ref[1, j] = later_ref[0, j]
        lam_ref[0, j] = adj_ref[0, j]
        gp_ref[j] = jnp.zeros((3 * Y, Z), F32)
        return carry

    lax.fori_loop(0, X, setup_row, 0)

    for i in range(fields):
        for k in range(1, NZL):
            z_copy(i, k).wait_recv()
        for side in range(2):
            x_copy(i, side).start()
        if i:
            for side in range(2):
                x_copy(i - 1, side).wait_recv()
                x_forward(i - 1, side).start()
    first_adjoint = field_pair(v_ref, 1, 0)

    def model_pair(i):
        m = m_ref.at[i]
        return Pair(m.at[8:12], m.at[0:4], m.at[4:8], m.at[12:16], ms_sem.at[i], mr_sem.at[i])

    def picked(load):
        total = pick_ref[0] * load(0)
        for a in range(1, PLACES):
            total = total + pick_ref[a] * load(a)
        return total

    def take(i):
        for side in range(2):
            x_forward(i, side).wait_recv()

        def row(j, carry):
            window = picked(lambda a: g_ref[i, j, 8 * a:8 * a + Y, :])
            if i == 0:
                cw_ref[j] = window
                v_ref[0, X + j, PAD:PAD + Y, :] = window * adj_ref[0, j]
            else:
                m_ref[i - 1, 4 + j] = window
            return carry

        lax.fori_loop(0, X, row, 0)
        if i == 0:
            first_adjoint.start()
        else:
            model_pair(i - 1).start()

    take(0)
    for side in range(2):
        x_copy(fields - 1, side).wait_recv()
        x_forward(fields - 1, side).start()
    for i in range(1, fields):
        take(i)
    for i in range(3):
        model_pair(i).wait_recv()

    def tensor_row(i, carry):
        outside = ((blk == 0) & (i < 4)) | ((blk == blocks - 1) & (i >= 12))
        twice = 2.0 * m_ref[0, i]
        tilt = m_ref[1, i]
        turn = m_ref[2, i]
        level, upright = sin_cos(tilt)
        half_sin, half_cos = sin_cos(0.5 * turn)
        e_ref[i] = twice
        e1_ref[i] = jnp.where(outside, 0.0, 1.0 + twice)
        nx_ref[i] = level * (1.0 - 2.0 * half_sin * half_sin)
        ny_ref[i] = level * (2.0 * half_sin * half_cos)
        nz_ref[i] = upright
        return carry

    lax.fori_loop(0, 2 * X, tensor_row, 0)

    matrix = mat_ref[...]

    def x_diff(ref, at):
        total = None
        for k in range(1, 5):
            term = COEF[k - 1] * (ref[at + k] - ref[at - k])
            total = term if total is None else total + term
        return total

    def operate(ref, p, finish):
        field = ref.at[p]

        def slope_z(h, carry):
            flat = field[pl.ds(4 + 4 * h, 4), PAD:PAD + Y, :].reshape(4 * Y, Z)
            slz_ref[pl.ds(4 * h, 4)] = depth_diff(flat, matrix).reshape(4, Y, Z)
            return carry

        lax.fori_loop(0, 4, slope_z, 0)

        def fluxes(i, own):
            slx = None
            sly = None
            for k in range(1, 5):
                tx = COEF[k - 1] * (field[i + 4 + k, PAD:PAD + Y, :] - field[i + 4 - k, PAD:PAD + Y, :])
                ty = COEF[k - 1] * (
                    field[i + 4, PAD + k:PAD + k + Y, :] - field[i + 4, PAD - k:PAD - k + Y, :]
                )
                slx = tx if slx is None else slx + tx
                sly = ty if sly is None else sly + ty
            slz = slz_ref[i]
            nx, ny, nz = nx_ref[i], ny_ref[i], nz_ref[i]
            pull = e_ref[i] * (nx * slx + ny * sly + nz * slz)
            e1 = e1_ref[i]
            fx_ref[i] = e1 * slx - nx * pull
            if own:
                fy_ref[i - 4, PAD:PAD + Y, :] = e1 * sly - ny * pull
                fz_ref[i - 4] = e1 * slz - nz * pull

        def halo_row(i, carry):
            fluxes(i, False)
            fluxes(i + 12, False)
            return carry

        def own_row(i, carry):
            fluxes(i + 4, True)
            return carry

        lax.fori_loop(0, 4, halo_row, 0)
        lax.fori_loop(0, X, own_row, 0)

        def flux_z(h, carry):
            flat = fz_ref[pl.ds(4 * h, 4)].reshape(4 * Y, Z)
            fz_ref[pl.ds(4 * h, 4)] = depth_diff(flat, matrix).reshape(4, Y, Z)
            return carry

        lax.fori_loop(0, 2, flux_z, 0)

        def result_row(j, carry):
            total = x_diff(fx_ref, j + 4)
            for k in range(1, 5):
                total = total + COEF[k - 1] * (
                    fy_ref[j, PAD + k:PAD + k + Y, :] - fy_ref[j, PAD - k:PAD - k + Y, :]
                )
            finish(j, total + fz_ref[j])
            return carry

        lax.fori_loop(0, X, result_row, 0)

    def reduce_copy(k):
        return remote(xs_ref.at[k - 1], xr_ref.at[k - 1], rs_sem.at[k - 1], rr_sem.at[k - 1], (shots_x[k - 1], blk))

    def spread_copy(k):
        rows = pl.ds(pl.multiple_of(((pz + k) % NZL) * 8, 8), 8)
        return remote(sum_ref.at[:, rows], zr_ref.at[k - 1], qs_sem.at[k - 1], qr_sem.at[k - 1], (shots_z[k - 1], blk))

    def chunk(j, target):
        return picked(lambda a: gp_ref[j, pl.ds(pl.multiple_of(Y + 32 * target - 8 * a, 8), 32), :])

    def round_(r, carry):
        p = lax.rem(r, 2)
        q = 1 - p
        coming = field_pair(u_ref, 0, p)
        coming.wait_recv()

        @pl.when(r < STEPS - 1)
        def _():
            amplitude = amp_ref[r]

            @pl.when(r > 0)
            def _():
                field_pair(u_ref, 0, q).wait_send()

            def finish(j, image):
                img_ref[r, j] = image
                current = u_ref[p, X + j, PAD:PAD + Y, :]
                u_ref[q, X + j, PAD:PAD + Y, :] = (
                    2.0 * current - old_ref[0, j] + cw_ref[j] * image + amplitude * at_ref[j]
                )
                old_ref[0, j] = current

            operate(u_ref, p, finish)
            field_pair(u_ref, 0, q).start()

        @pl.when(r == STEPS - 1)
        def _():
            def finish(j, image):
                grad = lam_ref[0, j] * image
                for t in range(STEPS - 1):
                    grad = grad + lam_ref[STEPS - 1 - t, j] * img_ref[t, j]
                gp_ref[j, Y:2 * Y, :] = grad

            operate(u_ref, p, finish)

            def pieces(j, carry):
                for k in range(1, NX):
                    xs_ref[k - 1, j] = chunk(j, (px + k) % NX)
                sum_ref[j] = chunk(j, px)
                return carry

            lax.fori_loop(0, X, pieces, 0)
            for k in range(1, NX):
                reduce_copy(k).start()

        field_pair(v_ref, 1, p).wait_recv()

        @pl.when((r > 0) & (r < STEPS - 1))
        def _():
            field_pair(v_ref, 1, q).wait_send()

        def finish_adjoint(j, image):
            present = lam_ref[r, j]
            earlier = 2.0 * present - old_ref[1, j] + image + inj_ref[STEPS - 1 - r, j]
            old_ref[1, j] = present
            lam_ref[r + 1, j] = earlier
            v_ref[q, X + j, PAD:PAD + Y, :] = cw_ref[j] * earlier

        @pl.when(r == STEPS - 1)
        def _():
            field_pair(v_ref, 1, q).wait_send()

        operate(v_ref, p, finish_adjoint)

        @pl.when(r < STEPS - 1)
        def _():
            field_pair(v_ref, 1, q).start()

        return carry

    lax.fori_loop(0, STEPS, round_, 0)

    for k in range(1, NX):
        reduce_copy(k).wait_recv()

    def total_row(j, carry):
        sum_ref[j] = sum_ref[j] + xr_ref[0, j] + xr_ref[1, j] + xr_ref[2, j]
        return carry

    lax.fori_loop(0, X, total_row, 0)
    for k in range(1, NZL):
        spread_copy(k).start()

    def out_row(j, carry):
        one_ref[0, j] = lam_ref[STEPS - 1, j]
        zero_ref[0, j] = lam_ref[STEPS, j]
        return carry

    lax.fori_loop(0, X, out_row, 0)
    for k in range(1, NZL):
        spread_copy(k).wait_recv()
    mine = pl.ds(pl.multiple_of(pz * 8, 8), 8)
    grad_ref[...] = sum_ref[:, mine, :] + zr_ref[0] + zr_ref[1] + zr_ref[2]

    for i in range(fields):
        for k in range(1, NZL):
            z_copy(i, k).wait_send()
        for side in range(2):
            x_copy(i, side).wait_send()
            x_forward(i, side).wait_send()
    for i in range(3):
        model_pair(i).wait_send()
    field_pair(u_ref, 0, 0).wait_send()
    field_pair(u_ref, 0, 1).wait_send()
    field_pair(v_ref, 1, 1).wait_send()
    for k in range(1, NX):
        reduce_copy(k).wait_send()
    for k in range(1, NZL):
        spread_copy(k).wait_send()


def on_device(
    blocks,
    state_before, state_now, adjoint_later, adjoint_now,
    courant_sq, epsilon, tilt_angle, azimuth,
    aperture_anchor, step_index, wavelet, residual_traces,
    source_x, source_y, source_z, receiver_x, receiver_y, receiver_z,
):
    block_index = lax.axis_index("blk")
    local_rows = receiver_x[0] - block_index * X
    plane_index = local_rows * Y + receiver_y[0]
    inside = (local_rows >= 0) & (local_rows < X)
    plane_pick = (
        (lax.broadcasted_iota(jnp.int32, (X * Y, plane_index.shape[0]), 0) == plane_index[None, :])
        & inside[None, :]
    ).astype(F32)
    samples = lax.dynamic_slice_in_dim(residual_traces[0], step_index[0], STEPS, axis=0)
    depth_match = (
        lax.broadcasted_iota(jnp.int32, (plane_index.shape[0], Z), 1) == receiver_z[0][:, None]
    ).astype(F32)
    injected = jnp.einsum(
        "pr,trz->tpz", plane_pick, depth_match[None] * samples[:, :, None],
        precision=lax.Precision.HIGHEST, preferred_element_type=F32,
    ).reshape(STEPS, X, Y, Z)

    amplitudes = lax.dynamic_slice_in_dim(wavelet[0], step_index[0], STEPS)
    pick = (aperture_anchor[0] == 8 * lax.broadcasted_iota(jnp.int32, (PLACES,), 0)).astype(F32)
    along = lambda axis: lax.broadcasted_iota(jnp.int32, (X, Y, Z), axis)
    source_at = (
        (along(0) == source_x[0] - block_index * X) & (along(1) == source_y[0]) & (along(2) == source_z[0])
    ).astype(F32)

    vmem = pl.BlockSpec(memory_space=pltpu.VMEM)
    smem = pl.BlockSpec(memory_space=pltpu.SMEM)
    v = lambda *shape: pltpu.VMEM(shape, F32)
    dma = lambda *shape: pltpu.SemaphoreType.DMA(shape)
    return pl.pallas_call(
        functools.partial(kernel, blocks),
        out_shape=(
            jax.ShapeDtypeStruct((1, X, Y, Z), F32),
            jax.ShapeDtypeStruct((1, X, Y, Z), F32),
            jax.ShapeDtypeStruct((X, 8, Z), F32),
        ),
        in_specs=[smem] * 2 + [vmem] * 11,
        out_specs=(vmem, vmem, vmem),
        scratch_shapes=[
            v(4, X, 128, Z), v(3, 2 * X, Y, Z),
            v(2, 3 * X, Y + 2 * PAD, Z), v(2, 3 * X, Y + 2 * PAD, Z),
            v(2, X, Y, Z), v(STEPS + 1, X, Y, Z), v(STEPS - 1, X, Y, Z), v(X, Y, Z),
            v(2 * X, Y, Z), v(2 * X, Y, Z), v(2 * X, Y, Z), v(2 * X, Y, Z), v(2 * X, Y, Z),
            v(2 * X, Y, Z), v(2 * X, Y, Z), v(X, Y + 2 * PAD, Z), v(X, Y, Z),
            v(X, 3 * Y, Z), v(3, X, 32, Z), v(3, X, 32, Z), v(X, 32, Z), v(3, X, 8, Z),
            dma(4, 3), dma(4, 3), dma(4, 2), dma(4, 2), dma(4, 2), dma(4, 2), dma(3, 2), dma(3, 2),
            dma(2, 2, 2), dma(2, 2, 2), dma(3), dma(3), dma(3), dma(3),
        ],
        compiler_params=pltpu.CompilerParams(
            collective_id=0, has_side_effects=True, vmem_limit_bytes=60000 * 1024,
        ),
    )(
        pick, amplitudes,
        state_before, state_now, adjoint_later, adjoint_now,
        courant_sq, epsilon, tilt_angle, azimuth, injected, source_at, depth_matrix(),
    )


def solution(mesh):
    field = P("shot", "blk", None, None)
    model = P("blk", "shot", None)
    in_specs = (
        (field,) * 4 + (model,) * 4
        + (P("shot"), P(), P("shot", None), P("shot", None, None))
        + (P("shot"),) * 3 + (P("shot", None),) * 3
    )
    return jax.shard_map(
        functools.partial(on_device, mesh.shape["blk"]),
        mesh=mesh, in_specs=in_specs, out_specs=(field, field, model), check_vma=False,
    )
```

```python
import functools
import math

import numpy as np
import jax
import jax.numpy as jnp
from jax import lax
from jax.experimental import pallas as pl
from jax.experimental.pallas import tpu as pltpu
from jax.sharding import PartitionSpec as P

STEPS = 4
COEF = (0.8, -0.2, 4.0 / 105.0, -1.0 / 280.0)
WHOLE = (672, -168, 32, -3)
MESH = pl.DeviceIdType.MESH
F32 = jnp.float32

X, Y, Z = 8, 64, 128
PAD = 8
PLACES = 9
NX, NZL = 4, 4


def depth_matrix():
    m = np.zeros((Z, Z), np.float32)
    for k in range(1, 5):
        for j in range(Z):
            if j + k < Z:
                m[j + k, j] += WHOLE[k - 1]
            if j - k >= 0:
                m[j - k, j] -= WHOLE[k - 1]
    return jnp.asarray(np.concatenate([m, m], 0), jnp.bfloat16)


def sin_cos(angle):
    square = angle * angle
    sine = jnp.full_like(angle, 1.0 / math.factorial(13))
    for n in (11, 9, 7, 5, 3, 1):
        sine = sine * square + (-1.0) ** (n // 2) / math.factorial(n)
    cosine = jnp.full_like(angle, -1.0 / math.factorial(14))
    for n in (12, 10, 8, 6, 4, 2, 0):
        cosine = cosine * square + (-1.0) ** (n // 2) / math.factorial(n)
    return sine * angle, cosine


def depth_diff(flat, matrix):
    upper = flat.astype(jnp.bfloat16)
    lower = (flat - upper.astype(F32)).astype(jnp.bfloat16)
    both = jnp.concatenate([upper, lower], axis=1)
    return jnp.dot(both, matrix, preferred_element_type=F32) * (1.0 / 840.0)


def kernel(
    blocks,
    anchor_ref, step_ref, sx_ref, sy_ref, sz_ref,
    wave_ref, residual_ref, rx_ref, ry_ref, rz_ref,
    before_ref, now_ref, later_ref, adj_ref,
    eps_ref, tilt_ref, az_ref, c_ref, mat_ref,
    one_ref, zero_ref, grad_ref,
    g_ref, m_ref, u_ref, v_ref, old_ref, lam_ref, img_ref, cw_ref,
    e1_ref, e_ref, nx_ref, ny_ref, nz_ref,
    slz_ref, fx_ref, fy_ref, fz_ref, src_ref, inj_ref, plane_ref,
    gp_ref, xs_ref, xr_ref, sum_ref, zr_ref,
    zs_sem, zr_sem, xs_sem, xr_sem, ms_sem, mr_sem,
    fs_sem, fr_sem, rs_sem, rr_sem, qs_sem, qr_sem,
):
    shot = lax.axis_index("shot")
    blk = lax.axis_index("blk")
    px = shot // NZL
    pz = shot % NZL
    has_left = blk > 0
    has_right = blk < blocks - 1
    shots_z = [px * NZL + (pz + k) % NZL for k in range(1, NZL)]
    shots_x = [((px + k) % NX) * NZL + pz for k in range(1, NX)]

    barrier = pltpu.get_barrier_semaphore()
    for other in shots_z + shots_x:
        pl.semaphore_signal(barrier, inc=1, device_id=(other, blk), device_id_type=MESH)

    @pl.when(has_left)
    def _():
        pl.semaphore_signal(barrier, inc=1, device_id=(shot, blk - 1), device_id_type=MESH)

    @pl.when(has_right)
    def _():
        pl.semaphore_signal(barrier, inc=1, device_id=(shot, blk + 1), device_id_type=MESH)

    peers = len(shots_z) + len(shots_x)

    @pl.when(has_left & has_right)
    def _():
        pl.semaphore_wait(barrier, peers + 2)

    @pl.when(jnp.logical_not(has_left & has_right))
    def _():
        pl.semaphore_wait(barrier, peers + 1)

    def remote(src, dst, ssem, rsem, device):
        return pltpu.make_async_remote_copy(
            src_ref=src, dst_ref=dst, send_sem=ssem, recv_sem=rsem,
            device_id=device, device_id_type=MESH,
        )

    class Pair:
        def __init__(self, src_right, dst_left_halo, src_left, dst_right_halo, ssem, rsem):
            self.right = remote(src_right, dst_left_halo, ssem.at[0], rsem.at[0], (shot, blk + 1))
            self.left = remote(src_left, dst_right_halo, ssem.at[1], rsem.at[1], (shot, blk - 1))

        def start(self):
            @pl.when(has_right)
            def _():
                self.right.start()

            @pl.when(has_left)
            def _():
                self.left.start()

        def wait_recv(self):
            @pl.when(has_left)
            def _():
                self.right.wait_recv()

            @pl.when(has_right)
            def _():
                self.left.wait_recv()

        def wait_send(self):
            @pl.when(has_right)
            def _():
                self.right.wait_send()

            @pl.when(has_left)
            def _():
                self.left.wait_send()

    def field_pair(ref, chain, p, src=None):
        own = ref.at[p, X:2 * X, PAD:PAD + Y] if src is None else src
        return Pair(
            own, ref.at[p, 0:X, PAD:PAD + Y], own, ref.at[p, 2 * X:3 * X, PAD:PAD + Y],
            fs_sem.at[chain, p], fr_sem.at[chain, p],
        )

    models = (eps_ref, tilt_ref, az_ref, c_ref)
    fields = len(models)

    def z_copy(i, k):
        rows = pl.ds(pl.multiple_of(shot * 8, 8), 8)
        return remote(models[i], g_ref.at[i, :, rows], zs_sem.at[i, k - 1], zr_sem.at[i, k - 1], (shots_z[k - 1], blk))

    def x_copy(i, k):
        rows = pl.ds(pl.multiple_of(px * 32, 8), 32)
        part = g_ref.at[i, :, rows]
        return remote(part, part, xs_sem.at[i, k - 1], xr_sem.at[i, k - 1], (shots_x[k - 1], blk))

    for i in range(fields):
        for k in range(1, NZL):
            z_copy(i, k).start()
    first_forward = field_pair(u_ref, 0, 0, now_ref.at[0])
    first_forward.start()

    own_rows = pl.ds(pl.multiple_of(shot * 8, 8), 8)
    for i in range(fields):
        g_ref[i, :, own_rows, :] = models[i][...]
    zeros_y = jnp.zeros((3 * X, PAD, Z), F32)
    for p in range(2):
        for ref in (u_ref, v_ref):
            ref[p, :, 0:PAD, :] = zeros_y
            ref[p, :, PAD + Y:, :] = zeros_y
    fy_ref[:, 0:PAD, :] = jnp.zeros((X, PAD, Z), F32)
    fy_ref[:, PAD + Y:, :] = jnp.zeros((X, PAD, Z), F32)

    def edge(at, m_at):
        def row(j, carry):
            for p in range(2):
                for ref in (u_ref, v_ref):
                    ref[p, at + j, PAD:PAD + Y, :] = jnp.zeros((Y, Z), F32)
            return carry

        lax.fori_loop(0, X, row, 0)

        def m_row(j, carry):
            for i in range(3):
                m_ref[i, m_at + j] = jnp.zeros((Y, Z), F32)
            return carry

        lax.fori_loop(0, 4, m_row, 0)

    @pl.when(blk == 0)
    def _():
        edge(0, 0)

    @pl.when(blk == blocks - 1)
    def _():
        edge(2 * X, 12)


    step = step_ref[0]
    anchor = jnp.full((Y, Z), anchor_ref[0], jnp.int32)
    row_y = lax.broadcasted_iota(jnp.int32, (Y, Z), 0)
    col_z = lax.broadcasted_iota(jnp.int32, (Y, Z), 1)
    at_yz = (row_y == sy_ref[0]) & (col_z == sz_ref[0])
    local_x = jnp.full((Y, Z), sx_ref[0] - blk * X, jnp.int32)
    times = lax.broadcasted_iota(jnp.int32, (1, 16), 1)
    amplitudes = [
        jnp.sum(jnp.where(times == step + t, wave_ref[...], 0.0), axis=1, keepdims=True)
        for t in range(STEPS - 1)
    ]

    def source_row(j, carry):
        here = at_yz & (local_x == j)
        for t in range(STEPS - 1):
            src_ref[t, j] = jnp.where(here, jnp.broadcast_to(amplitudes[t], (Y, Z)), 0.0)
        return carry

    def setup_row(j, carry):
        u_ref[0, X + j, PAD:PAD + Y, :] = now_ref[0, j]
        old_ref[0, j] = before_ref[0, j]
        old_ref[1, j] = later_ref[0, j]
        lam_ref[0, j] = adj_ref[0, j]
        gp_ref[j] = jnp.zeros((3 * Y, Z), F32)
        return carry

    lax.fori_loop(0, X, setup_row, 0)

    for i in range(fields):
        for k in range(1, NZL):
            z_copy(i, k).wait_recv()
        for k in (2, 1, 3):
            x_copy(i, k).start()
    first_adjoint = field_pair(v_ref, 1, 0)
    lax.fori_loop(0, X, source_row, 0)

    local_r = rx_ref[...] - blk * X

    def plane_row(j, carry):
        hit = (jnp.broadcast_to(ry_ref[...], (Y, Z)) == row_y) & (jnp.broadcast_to(local_r, (Y, Z)) == j)
        plane_ref[j] = jnp.where(hit, 1.0, 0.0)
        return carry

    lax.fori_loop(0, X, plane_row, 0)
    sample_row = lax.broadcasted_iota(jnp.int32, (16, Z), 0)
    depth_row = lax.broadcasted_iota(jnp.int32, (Z, Z), 0)
    at_depth = jnp.broadcast_to(rz_ref[...], (Z, Z)) == depth_row

    def inject(t, carry):
        samples = jnp.sum(jnp.where(sample_row == step + t, residual_ref[0], 0.0), axis=0, keepdims=True)
        rest = jnp.where(at_depth, jnp.broadcast_to(samples, (Z, Z)), 0.0)
        parts = []
        for _ in range(3):
            part = rest.astype(jnp.bfloat16)
            parts.append(part)
            rest = rest - part.astype(F32)
        depths = jnp.concatenate(parts, axis=1)
        for h in range(2):
            planes = plane_ref[4 * h:4 * h + 4].reshape(4 * Y, Z).astype(jnp.bfloat16)
            total = lax.dot_general(
                jnp.concatenate([planes] * 3, axis=1), depths, (((1,), (1,)), ((), ())),
                preferred_element_type=F32,
            )
            inj_ref[t, 4 * h:4 * h + 4] = total.reshape(4, Y, Z)
        return carry

    lax.fori_loop(0, STEPS, inject, 0)

    def model_pair(i):
        m = m_ref.at[i]
        return Pair(m.at[8:12], m.at[0:4], m.at[4:8], m.at[12:16], ms_sem.at[i], mr_sem.at[i])

    def picked(load, where):
        total = load(0)
        for a in range(1, PLACES):
            total = jnp.where(where == 8 * a, load(a), total)
        return total

    def take(i):
        for k in (1, 3, 2):
            x_copy(i, k).wait_recv()

        def row(j, carry):
            window = picked(lambda a: g_ref[i, j, 8 * a:8 * a + Y, :], anchor)
            if i == 3:
                cw_ref[j] = window
                v_ref[0, X + j, PAD:PAD + Y, :] = window * adj_ref[0, j]
            else:
                m_ref[i, 4 + j] = window
            return carry

        lax.fori_loop(0, X, row, 0)
        if i == 3:
            first_adjoint.start()
        else:
            model_pair(i).start()

    def tensor_row(i, carry):
        outside = ((blk == 0) & (i < 4)) | ((blk == blocks - 1) & (i >= 12))
        twice = 2.0 * m_ref[0, i]
        tilt = m_ref[1, i]
        turn = m_ref[2, i]
        level, upright = sin_cos(tilt)
        half_sin, half_cos = sin_cos(0.5 * turn)
        e_ref[i] = twice
        e1_ref[i] = jnp.where(outside, 0.0, 1.0 + twice)
        nx_ref[i] = level * (1.0 - 2.0 * half_sin * half_sin)
        ny_ref[i] = level * (2.0 * half_sin * half_cos)
        nz_ref[i] = upright
        return carry

    for i in range(3):
        take(i)
    lax.fori_loop(4, 12, tensor_row, 0)
    take(3)
    for i in range(3):
        model_pair(i).wait_recv()

    def tensor_halo(i, carry):
        tensor_row(i, carry)
        return tensor_row(i + 12, carry)

    lax.fori_loop(0, 4, tensor_halo, 0)

    matrix = mat_ref[...]

    def x_diff(ref, at):
        total = None
        for k in range(1, 5):
            term = COEF[k - 1] * (ref[at + k] - ref[at - k])
            total = term if total is None else total + term
        return total

    def operate(ref, p, finish):
        field = ref.at[p]

        def slope_z(h, carry):
            flat = field[pl.ds(4 + 4 * h, 4), PAD:PAD + Y, :].reshape(4 * Y, Z)
            slz_ref[pl.ds(4 * h, 4)] = depth_diff(flat, matrix).reshape(4, Y, Z)
            return carry

        lax.fori_loop(0, 4, slope_z, 0)

        def fluxes(i, own):
            slx = None
            sly = None
            for k in range(1, 5):
                tx = COEF[k - 1] * (field[i + 4 + k, PAD:PAD + Y, :] - field[i + 4 - k, PAD:PAD + Y, :])
                ty = COEF[k - 1] * (
                    field[i + 4, PAD + k:PAD + k + Y, :] - field[i + 4, PAD - k:PAD - k + Y, :]
                )
                slx = tx if slx is None else slx + tx
                sly = ty if sly is None else sly + ty
            slz = slz_ref[i]
            nx, ny, nz = nx_ref[i], ny_ref[i], nz_ref[i]
            pull = e_ref[i] * (nx * slx + ny * sly + nz * slz)
            e1 = e1_ref[i]
            fx_ref[i] = e1 * slx - nx * pull
            if own:
                fy_ref[i - 4, PAD:PAD + Y, :] = e1 * sly - ny * pull
                fz_ref[i - 4] = e1 * slz - nz * pull

        def halo_row(i, carry):
            fluxes(i, False)
            fluxes(i + 12, False)
            return carry

        def own_row(i, carry):
            fluxes(i + 4, True)
            return carry

        lax.fori_loop(0, 4, halo_row, 0)
        lax.fori_loop(0, X, own_row, 0)

        def flux_z(h, carry):
            flat = fz_ref[pl.ds(4 * h, 4)].reshape(4 * Y, Z)
            fz_ref[pl.ds(4 * h, 4)] = depth_diff(flat, matrix).reshape(4, Y, Z)
            return carry

        lax.fori_loop(0, 2, flux_z, 0)

        def result_row(j, carry):
            total = x_diff(fx_ref, j + 4)
            for k in range(1, 5):
                total = total + COEF[k - 1] * (
                    fy_ref[j, PAD + k:PAD + k + Y, :] - fy_ref[j, PAD - k:PAD - k + Y, :]
                )
            finish(j, total + fz_ref[j])
            return carry

        lax.fori_loop(0, X, result_row, 0)

    def reduce_copy(h, k):
        half = pl.ds(4 * h, 4)
        return remote(
            xs_ref.at[k - 1, half], xr_ref.at[k - 1, half], rs_sem.at[h, k - 1], rr_sem.at[h, k - 1],
            (shots_x[k - 1], blk),
        )

    def spread_copy(h, k):
        half = pl.ds(4 * h, 4)
        rows = pl.ds(pl.multiple_of(((pz + k) % NZL) * 8, 8), 8)
        return remote(
            sum_ref.at[half, rows], zr_ref.at[k - 1, half], qs_sem.at[h, k - 1], qr_sem.at[h, k - 1],
            (shots_z[k - 1], blk),
        )

    anchor_part = jnp.full((32, Z), anchor_ref[0], jnp.int32)

    def chunk(j, target):
        return picked(
            lambda a: gp_ref[j, pl.ds(pl.multiple_of(Y + 32 * target - 8 * a, 8), 32), :], anchor_part
        )

    def round_(r, carry):
        p = lax.rem(r, 2)
        q = 1 - p
        coming = field_pair(u_ref, 0, p)
        coming.wait_recv()

        @pl.when(r < STEPS - 1)
        def _():
            @pl.when(r > 0)
            def _():
                field_pair(u_ref, 0, q).wait_send()

            def finish(j, image):
                img_ref[r, j] = image
                current = u_ref[p, X + j, PAD:PAD + Y, :]
                u_ref[q, X + j, PAD:PAD + Y, :] = (
                    2.0 * current - old_ref[0, j] + cw_ref[j] * image + src_ref[r, j]
                )
                old_ref[0, j] = current

            operate(u_ref, p, finish)
            field_pair(u_ref, 0, q).start()

        @pl.when(r == STEPS - 1)
        def _():
            def finish(j, image):
                grad = lam_ref[0, j] * image
                for t in range(STEPS - 1):
                    grad = grad + lam_ref[STEPS - 1 - t, j] * img_ref[t, j]
                gp_ref[j, Y:2 * Y, :] = grad

            operate(u_ref, p, finish)

            def pieces(j, carry):
                for k in range(1, NX):
                    xs_ref[k - 1, j] = chunk(j, (px + k) % NX)
                sum_ref[j] = chunk(j, px)
                return carry

            for h in range(2):
                lax.fori_loop(4 * h, 4 * h + 4, pieces, 0)
                for k in (2, 1, 3):
                    reduce_copy(h, k).start()

        field_pair(v_ref, 1, p).wait_recv()

        @pl.when((r > 0) & (r < STEPS - 1))
        def _():
            field_pair(v_ref, 1, q).wait_send()

        def finish_adjoint(j, image):
            present = lam_ref[r, j]
            earlier = 2.0 * present - old_ref[1, j] + image + inj_ref[STEPS - 1 - r, j]
            old_ref[1, j] = present
            lam_ref[r + 1, j] = earlier
            v_ref[q, X + j, PAD:PAD + Y, :] = cw_ref[j] * earlier

        @pl.when(r == STEPS - 1)
        def _():
            field_pair(v_ref, 1, q).wait_send()

        operate(v_ref, p, finish_adjoint)

        @pl.when(r < STEPS - 1)
        def _():
            field_pair(v_ref, 1, q).start()

        return carry

    lax.fori_loop(0, STEPS, round_, 0)

    def total_row(j, carry):
        sum_ref[j] = sum_ref[j] + xr_ref[0, j] + xr_ref[1, j] + xr_ref[2, j]
        return carry

    for h in range(2):
        for k in range(1, NX):
            reduce_copy(h, k).wait_recv()
        lax.fori_loop(4 * h, 4 * h + 4, total_row, 0)
        for k in range(1, NZL):
            spread_copy(h, k).start()

    def out_row(j, carry):
        one_ref[0, j] = lam_ref[STEPS - 1, j]
        zero_ref[0, j] = lam_ref[STEPS, j]
        return carry

    lax.fori_loop(0, X, out_row, 0)
    for h in range(2):
        for k in range(1, NZL):
            spread_copy(h, k).wait_recv()
    mine = pl.ds(pl.multiple_of(pz * 8, 8), 8)
    grad_ref[...] = sum_ref[:, mine, :] + zr_ref[0] + zr_ref[1] + zr_ref[2]

    for i in range(fields):
        for k in range(1, NZL):
            z_copy(i, k).wait_send()
        for k in range(1, NX):
            x_copy(i, k).wait_send()
    for i in range(3):
        model_pair(i).wait_send()
    field_pair(u_ref, 0, 0).wait_send()
    field_pair(u_ref, 0, 1).wait_send()
    field_pair(v_ref, 1, 1).wait_send()
    for h in range(2):
        for k in range(1, NX):
            reduce_copy(h, k).wait_send()
        for k in range(1, NZL):
            spread_copy(h, k).wait_send()


def on_device(
    blocks,
    state_before, state_now, adjoint_later, adjoint_now,
    courant_sq, epsilon, tilt_angle, azimuth,
    aperture_anchor, step_index, wavelet, residual_traces,
    source_x, source_y, source_z, receiver_x, receiver_y, receiver_z,
):
    vmem = pl.BlockSpec(memory_space=pltpu.VMEM)
    smem = pl.BlockSpec(memory_space=pltpu.SMEM)
    v = lambda *shape: pltpu.VMEM(shape, F32)
    dma = lambda *shape: pltpu.SemaphoreType.DMA(shape)
    return pl.pallas_call(
        functools.partial(kernel, blocks),
        out_shape=(
            pltpu.VMEM((1, X, Y, Z), F32),
            pltpu.VMEM((1, X, Y, Z), F32),
            pltpu.VMEM((X, 8, Z), F32),
        ),
        in_specs=[smem] * 5 + [vmem] * 14,
        out_specs=(vmem, vmem, vmem),
        scratch_shapes=[
            v(4, X, 128, Z), v(3, 2 * X, Y, Z),
            v(2, 3 * X, Y + 2 * PAD, Z), v(2, 3 * X, Y + 2 * PAD, Z),
            v(2, X, Y, Z), v(STEPS + 1, X, Y, Z), v(STEPS - 1, X, Y, Z), v(X, Y, Z),
            v(2 * X, Y, Z), v(2 * X, Y, Z), v(2 * X, Y, Z), v(2 * X, Y, Z), v(2 * X, Y, Z),
            v(2 * X, Y, Z), v(2 * X, Y, Z), v(X, Y + 2 * PAD, Z), v(X, Y, Z),
            v(STEPS - 1, X, Y, Z), v(STEPS, X, Y, Z), v(X, Y, Z),
            v(X, 3 * Y, Z), v(3, X, 32, Z), v(3, X, 32, Z), v(X, 32, Z), v(3, X, 8, Z),
            dma(4, 3), dma(4, 3), dma(4, 3), dma(4, 3), dma(3, 2), dma(3, 2),
            dma(2, 2, 2), dma(2, 2, 2), dma(2, 3), dma(2, 3), dma(2, 3), dma(2, 3),
        ],
        compiler_params=pltpu.CompilerParams(
            collective_id=0, has_side_effects=True, vmem_limit_bytes=60000 * 1024,
        ),
    )(
        aperture_anchor, step_index, source_x, source_y, source_z,
        wavelet, residual_traces, receiver_x, receiver_y, receiver_z,
        state_before, state_now, adjoint_later, adjoint_now,
        epsilon, tilt_angle, azimuth, courant_sq, depth_matrix(),
    )


def solution(mesh):
    field = P("shot", "blk", None, None)
    model = P("blk", "shot", None)
    in_specs = (
        (field,) * 4 + (model,) * 4
        + (P("shot"), P(), P("shot", None), P("shot", None, None))
        + (P("shot"),) * 3 + (P("shot", None),) * 3
    )
    return jax.shard_map(
        functools.partial(on_device, mesh.shape["blk"]),
        mesh=mesh, in_specs=in_specs, out_specs=(field, field, model), check_vma=False,
    )
```

```python
import functools
import math

import numpy as np
import jax
import jax.numpy as jnp
from jax import lax
from jax.experimental import pallas as pl
from jax.experimental.pallas import tpu as pltpu
from jax.sharding import PartitionSpec as P

STEPS = 4
COEF = (0.8, -0.2, 4.0 / 105.0, -1.0 / 280.0)
WHOLE = (672, -168, 32, -3)
MESH = pl.DeviceIdType.MESH
F32 = jnp.float32

X, Y, Z = 8, 64, 128
PAD = 8
PLACES = 9
NX, NZL = 4, 4


def depth_matrix():
    m = np.zeros((Z, Z), np.float32)
    for k in range(1, 5):
        for j in range(Z):
            if j + k < Z:
                m[j + k, j] += WHOLE[k - 1]
            if j - k >= 0:
                m[j - k, j] -= WHOLE[k - 1]
    return jnp.asarray(np.concatenate([m, m], 0), jnp.bfloat16)


def sin_cos(angle):
    square = angle * angle
    sine = jnp.full_like(angle, 1.0 / math.factorial(13))
    for n in (11, 9, 7, 5, 3, 1):
        sine = sine * square + (-1.0) ** (n // 2) / math.factorial(n)
    cosine = jnp.full_like(angle, -1.0 / math.factorial(14))
    for n in (12, 10, 8, 6, 4, 2, 0):
        cosine = cosine * square + (-1.0) ** (n // 2) / math.factorial(n)
    return sine * angle, cosine


def depth_diff(flat, matrix):
    upper = flat.astype(jnp.bfloat16)
    lower = (flat - upper.astype(F32)).astype(jnp.bfloat16)
    both = jnp.concatenate([upper, lower], axis=1)
    return jnp.dot(both, matrix, preferred_element_type=F32) * (1.0 / 840.0)


def kernel(
    blocks,
    anchor_ref, step_ref, sx_ref, sy_ref, sz_ref,
    wave_ref, residual_ref, rx_ref, ry_ref, rz_ref,
    before_ref, now_ref, later_ref, adj_ref,
    eps_ref, tilt_ref, az_ref, c_ref, mat_ref,
    one_ref, zero_ref, grad_ref,
    g_ref, m_ref, u_ref, v_ref, old_ref, lam_ref, img_ref, cw_ref,
    e1_ref, e_ref, nx_ref, ny_ref, nz_ref,
    slz_ref, sly_ref, fx_ref, fy_ref, fz_ref, src_ref, inj_ref, plane_ref,
    gp_ref, xs_ref, xr_ref, sum_ref, zr_ref,
    go_sem, zs_sem, zr_sem, xs_sem, xr_sem, ms_sem, mr_sem,
    fs_sem, fr_sem, rs_sem, rr_sem, qs_sem, qr_sem,
):
    shot = lax.axis_index("shot")
    blk = lax.axis_index("blk")
    px = shot // NZL
    pz = shot % NZL
    has_left = blk > 0
    has_right = blk < blocks - 1
    seam = (blk == blocks // 2 - 1) | (blk == blocks // 2)
    mate = (blk == blocks // 2 - 2) | (blk == blocks // 2 + 1)
    shots_z = [px * NZL + (pz + k) % NZL for k in range(1, NZL)]
    shots_x = [((px + k) % NX) * NZL + pz for k in range(1, NX)]

    barrier = pltpu.get_barrier_semaphore()
    for other in shots_z + shots_x:
        pl.semaphore_signal(barrier, inc=1, device_id=(other, blk), device_id_type=MESH)

    @pl.when(has_left)
    def _():
        pl.semaphore_signal(barrier, inc=1, device_id=(shot, blk - 1), device_id_type=MESH)

    @pl.when(has_right)
    def _():
        pl.semaphore_signal(barrier, inc=1, device_id=(shot, blk + 1), device_id_type=MESH)

    peers = len(shots_z) + len(shots_x)

    @pl.when(has_left & has_right)
    def _():
        pl.semaphore_wait(barrier, peers + 2)

    @pl.when(jnp.logical_not(has_left & has_right))
    def _():
        pl.semaphore_wait(barrier, peers + 1)

    def remote(src, dst, ssem, rsem, device):
        return pltpu.make_async_remote_copy(
            src_ref=src, dst_ref=dst, send_sem=ssem, recv_sem=rsem,
            device_id=device, device_id_type=MESH,
        )

    class Pair:
        def __init__(self, src_right, dst_left_halo, src_left, dst_right_halo, ssem, rsem):
            self.right = remote(src_right, dst_left_halo, ssem.at[0], rsem.at[0], (shot, blk + 1))
            self.left = remote(src_left, dst_right_halo, ssem.at[1], rsem.at[1], (shot, blk - 1))

        def start(self):
            @pl.when(has_right)
            def _():
                self.right.start()

            @pl.when(has_left)
            def _():
                self.left.start()

        def wait_recv(self):
            @pl.when(has_left)
            def _():
                self.right.wait_recv()

            @pl.when(has_right)
            def _():
                self.left.wait_recv()

        def wait_send(self):
            @pl.when(has_right)
            def _():
                self.right.wait_send()

            @pl.when(has_left)
            def _():
                self.left.wait_send()

    def field_pair(ref, chain, p, src=None):
        own = ref.at[p, X:2 * X, PAD:PAD + Y] if src is None else src
        return Pair(
            own, ref.at[p, 0:X, PAD:PAD + Y], own, ref.at[p, 2 * X:3 * X, PAD:PAD + Y],
            fs_sem.at[chain, p], fr_sem.at[chain, p],
        )

    models = (eps_ref, tilt_ref, az_ref, c_ref)
    fields = len(models)

    def z_copy(i, k):
        rows = pl.ds(pl.multiple_of(shot * 8, 8), 8)
        return remote(models[i], g_ref.at[i, :, rows], zs_sem.at[i, k - 1], zr_sem.at[i, k - 1], (shots_z[k - 1], blk))

    def x_copy(i, k):
        rows = pl.ds(pl.multiple_of(px * 32, 8), 32)
        part = g_ref.at[i, :, rows]
        return remote(part, part, xs_sem.at[i, k - 1], xr_sem.at[i, k - 1], (shots_x[k - 1], blk))

    for i in range(fields):
        for k in range(1, NZL):
            z_copy(i, k).start()
    first_forward = field_pair(u_ref, 0, 0, now_ref.at[0])

    own_rows = pl.ds(pl.multiple_of(shot * 8, 8), 8)
    for i in range(fields):
        g_ref[i, :, own_rows, :] = models[i][...]
    zeros_y = jnp.zeros((3 * X, PAD, Z), F32)
    for p in range(2):
        for ref in (u_ref, v_ref):
            ref[p, :, 0:PAD, :] = zeros_y
            ref[p, :, PAD + Y:, :] = zeros_y
    fy_ref[:, 0:PAD, :] = jnp.zeros((X, PAD, Z), F32)
    fy_ref[:, PAD + Y:, :] = jnp.zeros((X, PAD, Z), F32)

    def edge(at, m_at):
        def row(j, carry):
            for p in range(2):
                for ref in (u_ref, v_ref):
                    ref[p, at + j, PAD:PAD + Y, :] = jnp.zeros((Y, Z), F32)
            return carry

        lax.fori_loop(0, X, row, 0)

        def m_row(j, carry):
            for i in range(3):
                m_ref[i, m_at + j] = jnp.zeros((Y, Z), F32)
            return carry

        lax.fori_loop(0, 4, m_row, 0)

    @pl.when(blk == 0)
    def _():
        edge(0, 0)

    @pl.when(blk == blocks - 1)
    def _():
        edge(2 * X, 12)


    step = step_ref[0]
    anchor = jnp.full((Y, Z), anchor_ref[0], jnp.int32)
    row_y = lax.broadcasted_iota(jnp.int32, (Y, Z), 0)
    col_z = lax.broadcasted_iota(jnp.int32, (Y, Z), 1)
    at_yz = (row_y == sy_ref[0]) & (col_z == sz_ref[0])
    local_x = jnp.full((Y, Z), sx_ref[0] - blk * X, jnp.int32)
    times = lax.broadcasted_iota(jnp.int32, (1, 16), 1)
    amplitudes = [
        jnp.sum(jnp.where(times == step + t, wave_ref[...], 0.0), axis=1, keepdims=True)
        for t in range(STEPS - 1)
    ]

    def source_row(j, carry):
        here = at_yz & (local_x == j)
        for t in range(STEPS - 1):
            src_ref[t, j] = jnp.where(here, jnp.broadcast_to(amplitudes[t], (Y, Z)), 0.0)
        return carry

    def setup_row(j, carry):
        u_ref[0, X + j, PAD:PAD + Y, :] = now_ref[0, j]
        old_ref[0, j] = before_ref[0, j]
        old_ref[1, j] = later_ref[0, j]
        lam_ref[0, j] = adj_ref[0, j]
        gp_ref[j] = jnp.zeros((3 * Y, Z), F32)
        return carry

    lax.fori_loop(0, X, setup_row, 0)

    for i in range(fields):
        for k in range(1, NZL):
            z_copy(i, k).wait_recv()
        if i == 0:
            @pl.when(mate)
            def _():
                pl.semaphore_wait(go_sem, 1)

        for k in (2, 1, 3):
            x_copy(i, k).start()
        if i == 1:
            first_forward.start()
    first_adjoint = field_pair(v_ref, 1, 0)
    lax.fori_loop(0, X, source_row, 0)

    local_r = rx_ref[...] - blk * X

    def plane_row(j, carry):
        hit = (jnp.broadcast_to(ry_ref[...], (Y, Z)) == row_y) & (jnp.broadcast_to(local_r, (Y, Z)) == j)
        plane_ref[j] = jnp.where(hit, 1.0, 0.0)
        return carry

    lax.fori_loop(0, X, plane_row, 0)
    sample_row = lax.broadcasted_iota(jnp.int32, (16, Z), 0)
    depth_row = lax.broadcasted_iota(jnp.int32, (Z, Z), 0)
    at_depth = jnp.broadcast_to(rz_ref[...], (Z, Z)) == depth_row

    def inject(t, carry):
        samples = jnp.sum(jnp.where(sample_row == step + t, residual_ref[0], 0.0), axis=0, keepdims=True)
        rest = jnp.where(at_depth, jnp.broadcast_to(samples, (Z, Z)), 0.0)
        parts = []
        for _ in range(3):
            part = rest.astype(jnp.bfloat16)
            parts.append(part)
            rest = rest - part.astype(F32)
        depths = jnp.concatenate(parts, axis=1)
        for h in range(2):
            planes = plane_ref[4 * h:4 * h + 4].reshape(4 * Y, Z).astype(jnp.bfloat16)
            total = lax.dot_general(
                jnp.concatenate([planes] * 3, axis=1), depths, (((1,), (1,)), ((), ())),
                preferred_element_type=F32,
            )
            inj_ref[t, 4 * h:4 * h + 4] = total.reshape(4, Y, Z)
        return carry

    lax.fori_loop(0, STEPS, inject, 0)

    @pl.when(seam)
    def _():
        for i in range(3):
            for k in range(1, NX):
                x_copy(i, k).wait_send()
        pl.semaphore_signal(go_sem, inc=1, device_id=(shot, blk + 1 - 2 * (blk % 2)), device_id_type=MESH)

    def model_pair(i):
        m = m_ref.at[i]
        return Pair(m.at[8:12], m.at[0:4], m.at[4:8], m.at[12:16], ms_sem.at[i], mr_sem.at[i])

    def picked(load, where):
        total = load(0)
        for a in range(1, PLACES):
            total = jnp.where(where == 8 * a, load(a), total)
        return total

    def take(i):
        for k in (1, 3, 2):
            x_copy(i, k).wait_recv()

        def row(j, carry):
            window = picked(lambda a: g_ref[i, j, 8 * a:8 * a + Y, :], anchor)
            if i == 3:
                cw_ref[j] = window
                v_ref[0, X + j, PAD:PAD + Y, :] = window * adj_ref[0, j]
            else:
                m_ref[i, 4 + j] = window
            return carry

        lax.fori_loop(0, X, row, 0)
        if i == 3:
            first_adjoint.start()
        else:
            model_pair(i).start()

    def tilt_row(i, carry):
        level, upright = sin_cos(m_ref[1, i])
        nx_ref[i] = level
        nz_ref[i] = upright
        return carry

    def tensor_row(i, carry):
        outside = ((blk == 0) & (i < 4)) | ((blk == blocks - 1) & (i >= 12))
        twice = 2.0 * m_ref[0, i]
        turn = m_ref[2, i]
        level = nx_ref[i]
        half_sin, half_cos = sin_cos(0.5 * turn)
        e_ref[i] = twice
        e1_ref[i] = jnp.where(outside, 0.0, 1.0 + twice)
        nx_ref[i] = level * (1.0 - 2.0 * half_sin * half_sin)
        ny_ref[i] = level * (2.0 * half_sin * half_cos)
        return carry

    for i in range(3):
        take(i)
    lax.fori_loop(4, 12, tilt_row, 0)
    lax.fori_loop(4, 12, tensor_row, 0)
    take(3)
    for i in range(2):
        model_pair(i).wait_recv()

    def tilt_halo(i, carry):
        tilt_row(i, carry)
        return tilt_row(i + 12, carry)

    lax.fori_loop(0, 4, tilt_halo, 0)
    model_pair(2).wait_recv()

    def tensor_halo(i, carry):
        tensor_row(i, carry)
        return tensor_row(i + 12, carry)

    lax.fori_loop(0, 4, tensor_halo, 0)

    matrix = mat_ref[...]

    def x_diff(ref, at):
        total = None
        for k in range(1, 5):
            term = COEF[k - 1] * (ref[at + k] - ref[at - k])
            total = term if total is None else total + term
        return total

    def slope_z(field, n, h):
        flat = field[pl.ds(4 + 4 * h, 4), PAD:PAD + Y, :].reshape(4 * Y, Z)
        slz_ref[n, pl.ds(4 * h, 4)] = depth_diff(flat, matrix).reshape(4, Y, Z)

    def slope_y(field, i):
        total = None
        for k in range(1, 5):
            term = COEF[k - 1] * (field[i, PAD + k:PAD + k + Y, :] - field[i, PAD - k:PAD - k + Y, :])
            total = term if total is None else total + term
        return total

    def prepare(ref, n, p):
        field = ref.at[p]
        slope_z(field, n, 1)
        slope_z(field, n, 2)

        def row(j, carry):
            sly_ref[n, j] = slope_y(field, X + j)
            return carry

        lax.fori_loop(0, X, row, 0)

    def operate(ref, n, p, finish):
        field = ref.at[p]
        slope_z(field, n, 0)
        slope_z(field, n, 3)

        def fluxes(i, own):
            slx = None
            for k in range(1, 5):
                tx = COEF[k - 1] * (field[i + 4 + k, PAD:PAD + Y, :] - field[i + 4 - k, PAD:PAD + Y, :])
                slx = tx if slx is None else slx + tx
            sly = sly_ref[n, i - 4] if own else slope_y(field, i + 4)
            slz = slz_ref[n, i]
            nx, ny, nz = nx_ref[i], ny_ref[i], nz_ref[i]
            pull = e_ref[i] * (nx * slx + ny * sly + nz * slz)
            e1 = e1_ref[i]
            fx_ref[i] = e1 * slx - nx * pull
            if own:
                fy_ref[i - 4, PAD:PAD + Y, :] = e1 * sly - ny * pull
                fz_ref[i - 4] = e1 * slz - nz * pull

        def halo_row(i, carry):
            fluxes(i, False)
            fluxes(i + 12, False)
            return carry

        def own_row(i, carry):
            fluxes(i + 4, True)
            return carry

        lax.fori_loop(0, 4, halo_row, 0)
        lax.fori_loop(0, X, own_row, 0)

        def flux_z(h, carry):
            flat = fz_ref[pl.ds(4 * h, 4)].reshape(4 * Y, Z)
            fz_ref[pl.ds(4 * h, 4)] = depth_diff(flat, matrix).reshape(4, Y, Z)
            return carry

        lax.fori_loop(0, 2, flux_z, 0)

        def result_row(j, carry):
            total = x_diff(fx_ref, j + 4)
            for k in range(1, 5):
                total = total + COEF[k - 1] * (
                    fy_ref[j, PAD + k:PAD + k + Y, :] - fy_ref[j, PAD - k:PAD - k + Y, :]
                )
            finish(j, total + fz_ref[j])
            return carry

        lax.fori_loop(0, X, result_row, 0)

    def reduce_copy(h, k):
        half = pl.ds(4 * h, 4)
        return remote(
            xs_ref.at[k - 1, half], xr_ref.at[k - 1, half], rs_sem.at[h, k - 1], rr_sem.at[h, k - 1],
            (shots_x[k - 1], blk),
        )

    def spread_copy(h, k):
        half = pl.ds(4 * h, 4)
        rows = pl.ds(pl.multiple_of(((pz + k) % NZL) * 8, 8), 8)
        return remote(
            sum_ref.at[half, rows], zr_ref.at[k - 1, half], qs_sem.at[h, k - 1], qr_sem.at[h, k - 1],
            (shots_z[k - 1], blk),
        )

    anchor_part = jnp.full((32, Z), anchor_ref[0], jnp.int32)

    def chunk(j, target):
        return picked(
            lambda a: gp_ref[j, pl.ds(pl.multiple_of(Y + 32 * target - 8 * a, 8), 32), :], anchor_part
        )

    def round_(r, carry):
        p = lax.rem(r, 2)
        q = 1 - p
        coming = field_pair(u_ref, 0, p)
        prepare(u_ref, 0, p)
        coming.wait_recv()

        @pl.when(r < STEPS - 1)
        def _():
            @pl.when(r > 0)
            def _():
                field_pair(u_ref, 0, q).wait_send()

            def finish(j, image):
                img_ref[r, j] = image
                current = u_ref[p, X + j, PAD:PAD + Y, :]
                u_ref[q, X + j, PAD:PAD + Y, :] = (
                    2.0 * current - old_ref[0, j] + cw_ref[j] * image + src_ref[r, j]
                )
                old_ref[0, j] = current

            operate(u_ref, 0, p, finish)
            field_pair(u_ref, 0, q).start()

        @pl.when(r == STEPS - 1)
        def _():
            def finish(j, image):
                grad = lam_ref[0, j] * image
                for t in range(STEPS - 1):
                    grad = grad + lam_ref[STEPS - 1 - t, j] * img_ref[t, j]
                gp_ref[j, Y:2 * Y, :] = grad

            operate(u_ref, 0, p, finish)

            def pieces(j, carry):
                for k in range(1, NX):
                    xs_ref[k - 1, j] = chunk(j, (px + k) % NX)
                sum_ref[j] = chunk(j, px)
                return carry

            for h in range(2):
                lax.fori_loop(4 * h, 4 * h + 4, pieces, 0)
                for k in (2, 1, 3):
                    reduce_copy(h, k).start()

        prepare(v_ref, 1, p)
        field_pair(v_ref, 1, p).wait_recv()

        @pl.when((r > 0) & (r < STEPS - 1))
        def _():
            field_pair(v_ref, 1, q).wait_send()

        def finish_adjoint(j, image):
            present = lam_ref[r, j]
            earlier = 2.0 * present - old_ref[1, j] + image + inj_ref[STEPS - 1 - r, j]
            old_ref[1, j] = present
            lam_ref[r + 1, j] = earlier
            v_ref[q, X + j, PAD:PAD + Y, :] = cw_ref[j] * earlier

        @pl.when(r == STEPS - 1)
        def _():
            field_pair(v_ref, 1, q).wait_send()

        operate(v_ref, 1, p, finish_adjoint)

        @pl.when(r < STEPS - 1)
        def _():
            field_pair(v_ref, 1, q).start()

        return carry

    lax.fori_loop(0, STEPS, round_, 0)

    def total_row(j, carry):
        sum_ref[j] = sum_ref[j] + xr_ref[0, j] + xr_ref[1, j] + xr_ref[2, j]
        return carry

    for h in range(2):
        for k in range(1, NX):
            reduce_copy(h, k).wait_recv()
        lax.fori_loop(4 * h, 4 * h + 4, total_row, 0)
        for k in range(1, NZL):
            spread_copy(h, k).start()

    def out_row(j, carry):
        one_ref[0, j] = lam_ref[STEPS - 1, j]
        zero_ref[0, j] = lam_ref[STEPS, j]
        return carry

    lax.fori_loop(0, X, out_row, 0)
    for h in range(2):
        for k in range(1, NZL):
            spread_copy(h, k).wait_recv()
    mine = pl.ds(pl.multiple_of(pz * 8, 8), 8)
    grad_ref[...] = sum_ref[:, mine, :] + zr_ref[0] + zr_ref[1] + zr_ref[2]

    for i in range(fields):
        for k in range(1, NZL):
            z_copy(i, k).wait_send()

    @pl.when(jnp.logical_not(seam))
    def _():
        for i in range(3):
            for k in range(1, NX):
                x_copy(i, k).wait_send()

    for k in range(1, NX):
        x_copy(3, k).wait_send()
    for i in range(3):
        model_pair(i).wait_send()
    field_pair(u_ref, 0, 0).wait_send()
    field_pair(u_ref, 0, 1).wait_send()
    field_pair(v_ref, 1, 1).wait_send()
    for h in range(2):
        for k in range(1, NX):
            reduce_copy(h, k).wait_send()
        for k in range(1, NZL):
            spread_copy(h, k).wait_send()


def on_device(
    blocks,
    state_before, state_now, adjoint_later, adjoint_now,
    courant_sq, epsilon, tilt_angle, azimuth,
    aperture_anchor, step_index, wavelet, residual_traces,
    source_x, source_y, source_z, receiver_x, receiver_y, receiver_z,
):
    vmem = pl.BlockSpec(memory_space=pltpu.VMEM)
    smem = pl.BlockSpec(memory_space=pltpu.SMEM)
    v = lambda *shape: pltpu.VMEM(shape, F32)
    dma = lambda *shape: pltpu.SemaphoreType.DMA(shape)
    return pl.pallas_call(
        functools.partial(kernel, blocks),
        out_shape=(
            pltpu.VMEM((1, X, Y, Z), F32),
            pltpu.VMEM((1, X, Y, Z), F32),
            pltpu.VMEM((X, 8, Z), F32),
        ),
        in_specs=[smem] * 5 + [vmem] * 14,
        out_specs=(vmem, vmem, vmem),
        scratch_shapes=[
            v(4, X, 128, Z), v(3, 2 * X, Y, Z),
            v(2, 3 * X, Y + 2 * PAD, Z), v(2, 3 * X, Y + 2 * PAD, Z),
            v(2, X, Y, Z), v(STEPS + 1, X, Y, Z), v(STEPS - 1, X, Y, Z), v(X, Y, Z),
            v(2 * X, Y, Z), v(2 * X, Y, Z), v(2 * X, Y, Z), v(2 * X, Y, Z), v(2 * X, Y, Z),
            v(2, 2 * X, Y, Z), v(2, X, Y, Z), v(2 * X, Y, Z), v(X, Y + 2 * PAD, Z), v(X, Y, Z),
            v(STEPS - 1, X, Y, Z), v(STEPS, X, Y, Z), v(X, Y, Z),
            v(X, 3 * Y, Z), v(3, X, 32, Z), v(3, X, 32, Z), v(X, 32, Z), v(3, X, 8, Z),
            pltpu.SemaphoreType.REGULAR, dma(4, 3), dma(4, 3), dma(4, 3), dma(4, 3), dma(3, 2), dma(3, 2),
            dma(2, 2, 2), dma(2, 2, 2), dma(2, 3), dma(2, 3), dma(2, 3), dma(2, 3),
        ],
        compiler_params=pltpu.CompilerParams(
            collective_id=0, has_side_effects=True, vmem_limit_bytes=60000 * 1024,
        ),
    )(
        aperture_anchor, step_index, source_x, source_y, source_z,
        wavelet, residual_traces, receiver_x, receiver_y, receiver_z,
        state_before, state_now, adjoint_later, adjoint_now,
        epsilon, tilt_angle, azimuth, courant_sq, depth_matrix(),
    )


def solution(mesh):
    field = P("shot", "blk", None, None)
    model = P("blk", "shot", None)
    in_specs = (
        (field,) * 4 + (model,) * 4
        + (P("shot"), P(), P("shot", None), P("shot", None, None))
        + (P("shot"),) * 3 + (P("shot", None),) * 3
    )
    return jax.shard_map(
        functools.partial(on_device, mesh.shape["blk"]),
        mesh=mesh, in_specs=in_specs, out_specs=(field, field, model), check_vma=False,
    )
```

```python
import functools
import math

import numpy as np
import jax
import jax.numpy as jnp
from jax import lax
from jax.experimental import pallas as pl
from jax.experimental.pallas import tpu as pltpu
from jax.sharding import PartitionSpec as P

STEPS = 4
COEF = (0.8, -0.2, 4.0 / 105.0, -1.0 / 280.0)
WHOLE = (672, -168, 32, -3)
MESH = pl.DeviceIdType.MESH
F32 = jnp.float32

X, Y, Z = 8, 64, 128
PAD = 8
PLACES = 9
NX, NZL = 4, 4


def depth_matrix():
    m = np.zeros((Z, Z), np.float32)
    for k in range(1, 5):
        for j in range(Z):
            if j + k < Z:
                m[j + k, j] += WHOLE[k - 1]
            if j - k >= 0:
                m[j - k, j] -= WHOLE[k - 1]
    return jnp.asarray(np.concatenate([m, m], 0), jnp.bfloat16)


def sin_cos(angle):
    square = angle * angle
    sine = jnp.full_like(angle, 1.0 / math.factorial(13))
    for n in (11, 9, 7, 5, 3, 1):
        sine = sine * square + (-1.0) ** (n // 2) / math.factorial(n)
    cosine = jnp.full_like(angle, -1.0 / math.factorial(14))
    for n in (12, 10, 8, 6, 4, 2, 0):
        cosine = cosine * square + (-1.0) ** (n // 2) / math.factorial(n)
    return sine * angle, cosine


def depth_diff(flat, matrix):
    upper = flat.astype(jnp.bfloat16)
    lower = (flat - upper.astype(F32)).astype(jnp.bfloat16)
    both = jnp.concatenate([upper, lower], axis=1)
    return jnp.dot(both, matrix, preferred_element_type=F32) * (1.0 / 840.0)


def kernel(
    blocks,
    anchor_ref, step_ref, sx_ref, sy_ref, sz_ref,
    wave_ref, residual_ref, rx_ref, ry_ref, rz_ref,
    before_ref, now_ref, later_ref, adj_ref,
    eps_ref, tilt_ref, az_ref, c_ref, mat_ref,
    one_ref, zero_ref, grad_ref,
    g_ref, m_ref, u_ref, v_ref, old_ref, lam_ref, img_ref, cw_ref,
    e1_ref, e_ref, nx_ref, ny_ref, nz_ref,
    slz_ref, sly_ref, fx_ref, fy_ref, fz_ref, src_ref, inj_ref, plane_ref,
    gp_ref, xs_ref, xr_ref, sum_ref, zr_ref,
    go_sem, zs_sem, zr_sem, xs_sem, xr_sem, ms_sem, mr_sem,
    fs_sem, fr_sem, rs_sem, rr_sem, qs_sem, qr_sem,
):
    shot = lax.axis_index("shot")
    blk = lax.axis_index("blk")
    px = shot // NZL
    pz = shot % NZL
    has_left = blk > 0
    has_right = blk < blocks - 1
    seam = (blk == blocks // 2 - 1) | (blk == blocks // 2)
    mate = (blk == blocks // 2 - 2) | (blk == blocks // 2 + 1)
    shots_z = [px * NZL + (pz + k) % NZL for k in range(1, NZL)]
    shots_x = [((px + k) % NX) * NZL + pz for k in range(1, NX)]

    barrier = pltpu.get_barrier_semaphore()
    for other in shots_z + shots_x:
        pl.semaphore_signal(barrier, inc=1, device_id=(other, blk), device_id_type=MESH)

    @pl.when(has_left)
    def _():
        pl.semaphore_signal(barrier, inc=1, device_id=(shot, blk - 1), device_id_type=MESH)

    @pl.when(has_right)
    def _():
        pl.semaphore_signal(barrier, inc=1, device_id=(shot, blk + 1), device_id_type=MESH)

    peers = len(shots_z) + len(shots_x)

    @pl.when(has_left & has_right)
    def _():
        pl.semaphore_wait(barrier, peers + 2)

    @pl.when(jnp.logical_not(has_left & has_right))
    def _():
        pl.semaphore_wait(barrier, peers + 1)

    def remote(src, dst, ssem, rsem, device):
        return pltpu.make_async_remote_copy(
            src_ref=src, dst_ref=dst, send_sem=ssem, recv_sem=rsem,
            device_id=device, device_id_type=MESH,
        )

    class Pair:
        def __init__(self, src_right, dst_left_halo, src_left, dst_right_halo, ssem, rsem):
            self.right = remote(src_right, dst_left_halo, ssem.at[0], rsem.at[0], (shot, blk + 1))
            self.left = remote(src_left, dst_right_halo, ssem.at[1], rsem.at[1], (shot, blk - 1))

        def start(self):
            @pl.when(has_right)
            def _():
                self.right.start()

            @pl.when(has_left)
            def _():
                self.left.start()

        def wait_recv(self):
            @pl.when(has_left)
            def _():
                self.right.wait_recv()

            @pl.when(has_right)
            def _():
                self.left.wait_recv()

        def wait_send(self):
            @pl.when(has_right)
            def _():
                self.right.wait_send()

            @pl.when(has_left)
            def _():
                self.left.wait_send()

    def field_pair(ref, chain, p, src=None):
        own = ref.at[p, X:2 * X, PAD:PAD + Y] if src is None else src
        return Pair(
            own, ref.at[p, 0:X, PAD:PAD + Y], own, ref.at[p, 2 * X:3 * X, PAD:PAD + Y],
            fs_sem.at[chain, p], fr_sem.at[chain, p],
        )

    models = (eps_ref, tilt_ref, az_ref, c_ref)
    fields = len(models)

    def z_copy(i, k):
        rows = pl.ds(pl.multiple_of(shot * 8, 8), 8)
        return remote(models[i], g_ref.at[i, :, rows], zs_sem.at[i, k - 1], zr_sem.at[i, k - 1], (shots_z[k - 1], blk))

    def x_copy(i, k):
        rows = pl.ds(pl.multiple_of(px * 32, 8), 32)
        part = g_ref.at[i, :, rows]
        return remote(part, part, xs_sem.at[i, k - 1], xr_sem.at[i, k - 1], (shots_x[k - 1], blk))

    for i in range(fields):
        for k in range(1, NZL):
            z_copy(i, k).start()
    first_forward = field_pair(u_ref, 0, 0, now_ref.at[0])

    own_rows = pl.ds(pl.multiple_of(shot * 8, 8), 8)
    for i in range(fields):
        g_ref[i, :, own_rows, :] = models[i][...]
    zeros_y = jnp.zeros((3 * X, PAD, Z), F32)
    for p in range(2):
        for ref in (u_ref, v_ref):
            ref[p, :, 0:PAD, :] = zeros_y
            ref[p, :, PAD + Y:, :] = zeros_y
    fy_ref[:, 0:PAD, :] = jnp.zeros((X, PAD, Z), F32)
    fy_ref[:, PAD + Y:, :] = jnp.zeros((X, PAD, Z), F32)

    def edge(at, m_at):
        def row(j, carry):
            for p in range(2):
                for ref in (u_ref, v_ref):
                    ref[p, at + j, PAD:PAD + Y, :] = jnp.zeros((Y, Z), F32)
            return carry

        lax.fori_loop(0, X, row, 0)

        def m_row(j, carry):
            for i in range(3):
                m_ref[i, m_at + j] = jnp.zeros((Y, Z), F32)
            return carry

        lax.fori_loop(0, 4, m_row, 0)

    @pl.when(blk == 0)
    def _():
        edge(0, 0)

    @pl.when(blk == blocks - 1)
    def _():
        edge(2 * X, 12)


    step = step_ref[0]
    anchor = jnp.full((Y, Z), anchor_ref[0], jnp.int32)
    row_y = lax.broadcasted_iota(jnp.int32, (Y, Z), 0)
    col_z = lax.broadcasted_iota(jnp.int32, (Y, Z), 1)
    at_yz = (row_y == sy_ref[0]) & (col_z == sz_ref[0])
    local_x = jnp.full((Y, Z), sx_ref[0] - blk * X, jnp.int32)
    times = lax.broadcasted_iota(jnp.int32, (1, 16), 1)
    amplitudes = [
        jnp.sum(jnp.where(times == step + t, wave_ref[...], 0.0), axis=1, keepdims=True)
        for t in range(STEPS - 1)
    ]

    def source_row(j, carry):
        here = at_yz & (local_x == j)
        for t in range(STEPS - 1):
            src_ref[t, j] = jnp.where(here, jnp.broadcast_to(amplitudes[t], (Y, Z)), 0.0)
        return carry

    def setup_row(j, carry):
        u_ref[0, X + j, PAD:PAD + Y, :] = now_ref[0, j]
        old_ref[0, j] = before_ref[0, j]
        old_ref[1, j] = later_ref[0, j]
        lam_ref[0, j] = adj_ref[0, j]
        gp_ref[j] = jnp.zeros((3 * Y, Z), F32)
        return carry

    lax.fori_loop(0, X, setup_row, 0)

    for i in range(fields):
        for k in range(1, NZL):
            z_copy(i, k).wait_recv()
        if i == 0:
            @pl.when(mate)
            def _():
                pl.semaphore_wait(go_sem, 1)

        for k in (2, 1, 3):
            x_copy(i, k).start()
        if i == 1:
            first_forward.start()
    first_adjoint = field_pair(v_ref, 1, 0)

    local_r = rx_ref[...] - blk * X

    def plane_row(j, carry):
        hit = (jnp.broadcast_to(ry_ref[...], (Y, Z)) == row_y) & (jnp.broadcast_to(local_r, (Y, Z)) == j)
        plane_ref[j] = jnp.where(hit, 1.0, 0.0)
        return carry

    sample_row = lax.broadcasted_iota(jnp.int32, (16, Z), 0)
    depth_row = lax.broadcasted_iota(jnp.int32, (Z, Z), 0)
    at_depth = jnp.broadcast_to(rz_ref[...], (Z, Z)) == depth_row

    def inject(t, carry):
        samples = jnp.sum(jnp.where(sample_row == step + t, residual_ref[0], 0.0), axis=0, keepdims=True)
        rest = jnp.where(at_depth, jnp.broadcast_to(samples, (Z, Z)), 0.0)
        parts = []
        for _ in range(3):
            part = rest.astype(jnp.bfloat16)
            parts.append(part)
            rest = rest - part.astype(F32)
        depths = jnp.concatenate(parts, axis=1)
        for h in range(2):
            planes = plane_ref[4 * h:4 * h + 4].reshape(4 * Y, Z).astype(jnp.bfloat16)
            total = lax.dot_general(
                jnp.concatenate([planes] * 3, axis=1), depths, (((1,), (1,)), ((), ())),
                preferred_element_type=F32,
            )
            inj_ref[t, 4 * h:4 * h + 4] = total.reshape(4, Y, Z)
        return carry

    def set_sources():
        lax.fori_loop(0, X, source_row, 0)
        lax.fori_loop(0, X, plane_row, 0)
        lax.fori_loop(0, STEPS, inject, 0)

    @pl.when(seam)
    def _():
        for i in range(3):
            for k in range(1, NX):
                x_copy(i, k).wait_send()
        pl.semaphore_signal(go_sem, inc=1, device_id=(shot, blk + 1 - 2 * (blk % 2)), device_id_type=MESH)

    @pl.when(jnp.logical_not(seam))
    def _():
        set_sources()

    def model_pair(i):
        m = m_ref.at[i]
        return Pair(m.at[8:12], m.at[0:4], m.at[4:8], m.at[12:16], ms_sem.at[i], mr_sem.at[i])

    def picked(load, where):
        total = load(0)
        for a in range(1, PLACES):
            total = jnp.where(where == 8 * a, load(a), total)
        return total

    def take(i):
        for k in (1, 3, 2):
            x_copy(i, k).wait_recv()

        def row(j, carry):
            window = picked(lambda a: g_ref[i, j, 8 * a:8 * a + Y, :], anchor)
            if i == 3:
                cw_ref[j] = window
                v_ref[0, X + j, PAD:PAD + Y, :] = window * adj_ref[0, j]
            else:
                m_ref[i, 4 + j] = window
            return carry

        lax.fori_loop(0, X, row, 0)
        if i == 3:
            first_adjoint.start()
        else:
            model_pair(i).start()

    def tilt_row(i, carry):
        level, upright = sin_cos(m_ref[1, i])
        nx_ref[i] = level
        nz_ref[i] = upright
        return carry

    def tensor_row(i, carry):
        outside = ((blk == 0) & (i < 4)) | ((blk == blocks - 1) & (i >= 12))
        twice = 2.0 * m_ref[0, i]
        turn = m_ref[2, i]
        level = nx_ref[i]
        half_sin, half_cos = sin_cos(0.5 * turn)
        e_ref[i] = twice
        e1_ref[i] = jnp.where(outside, 0.0, 1.0 + twice)
        nx_ref[i] = level * (1.0 - 2.0 * half_sin * half_sin)
        ny_ref[i] = level * (2.0 * half_sin * half_cos)
        return carry

    for i in range(3):
        take(i)
    lax.fori_loop(4, 12, tilt_row, 0)
    lax.fori_loop(4, 12, tensor_row, 0)
    take(3)

    @pl.when(seam)
    def _():
        set_sources()

    for i in range(2):
        model_pair(i).wait_recv()

    def tilt_halo(i, carry):
        tilt_row(i, carry)
        return tilt_row(i + 12, carry)

    lax.fori_loop(0, 4, tilt_halo, 0)
    model_pair(2).wait_recv()

    def tensor_halo(i, carry):
        tensor_row(i, carry)
        return tensor_row(i + 12, carry)

    lax.fori_loop(0, 4, tensor_halo, 0)

    matrix = mat_ref[...]

    def x_diff(ref, at):
        total = None
        for k in range(1, 5):
            term = COEF[k - 1] * (ref[at + k] - ref[at - k])
            total = term if total is None else total + term
        return total

    def slope_z(field, n, h):
        flat = field[pl.ds(4 + 4 * h, 4), PAD:PAD + Y, :].reshape(4 * Y, Z)
        slz_ref[n, pl.ds(4 * h, 4)] = depth_diff(flat, matrix).reshape(4, Y, Z)

    def slope_y(field, i):
        total = None
        for k in range(1, 5):
            term = COEF[k - 1] * (field[i, PAD + k:PAD + k + Y, :] - field[i, PAD - k:PAD - k + Y, :])
            total = term if total is None else total + term
        return total

    def prepare(ref, n, p):
        field = ref.at[p]
        slope_z(field, n, 1)
        slope_z(field, n, 2)

        def row(j, carry):
            sly_ref[n, j] = slope_y(field, X + j)
            return carry

        lax.fori_loop(0, X, row, 0)

    def operate(ref, n, p, finish):
        field = ref.at[p]
        slope_z(field, n, 0)
        slope_z(field, n, 3)

        def fluxes(i, own):
            slx = None
            for k in range(1, 5):
                tx = COEF[k - 1] * (field[i + 4 + k, PAD:PAD + Y, :] - field[i + 4 - k, PAD:PAD + Y, :])
                slx = tx if slx is None else slx + tx
            sly = sly_ref[n, i - 4] if own else slope_y(field, i + 4)
            slz = slz_ref[n, i]
            nx, ny, nz = nx_ref[i], ny_ref[i], nz_ref[i]
            pull = e_ref[i] * (nx * slx + ny * sly + nz * slz)
            e1 = e1_ref[i]
            fx_ref[i] = e1 * slx - nx * pull
            if own:
                fy_ref[i - 4, PAD:PAD + Y, :] = e1 * sly - ny * pull
                fz_ref[i - 4] = e1 * slz - nz * pull

        def halo_row(i, carry):
            fluxes(i, False)
            fluxes(i + 12, False)
            return carry

        def own_row(i, carry):
            fluxes(i + 4, True)
            return carry

        lax.fori_loop(0, 4, halo_row, 0)
        lax.fori_loop(0, X, own_row, 0)

        def flux_z(h, carry):
            flat = fz_ref[pl.ds(4 * h, 4)].reshape(4 * Y, Z)
            fz_ref[pl.ds(4 * h, 4)] = depth_diff(flat, matrix).reshape(4, Y, Z)
            return carry

        lax.fori_loop(0, 2, flux_z, 0)

        def result_row(j, carry):
            total = x_diff(fx_ref, j + 4)
            for k in range(1, 5):
                total = total + COEF[k - 1] * (
                    fy_ref[j, PAD + k:PAD + k + Y, :] - fy_ref[j, PAD - k:PAD - k + Y, :]
                )
            finish(j, total + fz_ref[j])
            return carry

        lax.fori_loop(0, X, result_row, 0)

    def reduce_copy(h, k):
        half = pl.ds(4 * h, 4)
        return remote(
            xs_ref.at[k - 1, half], xr_ref.at[k - 1, half], rs_sem.at[h, k - 1], rr_sem.at[h, k - 1],
            (shots_x[k - 1], blk),
        )

    def spread_copy(h, k):
        half = pl.ds(4 * h, 4)
        rows = pl.ds(pl.multiple_of(((pz + k) % NZL) * 8, 8), 8)
        return remote(
            sum_ref.at[half, rows], zr_ref.at[k - 1, half], qs_sem.at[h, k - 1], qr_sem.at[h, k - 1],
            (shots_z[k - 1], blk),
        )

    anchor_part = jnp.full((32, Z), anchor_ref[0], jnp.int32)

    def chunk(j, target):
        return picked(
            lambda a: gp_ref[j, pl.ds(pl.multiple_of(Y + 32 * target - 8 * a, 8), 32), :], anchor_part
        )

    def round_(r, carry):
        p = lax.rem(r, 2)
        q = 1 - p
        coming = field_pair(u_ref, 0, p)
        prepare(u_ref, 0, p)
        coming.wait_recv()

        @pl.when(r < STEPS - 1)
        def _():
            def finish(j, image):
                img_ref[r, j] = image
                current = u_ref[p, X + j, PAD:PAD + Y, :]
                u_ref[q, X + j, PAD:PAD + Y, :] = (
                    2.0 * current - old_ref[0, j] + cw_ref[j] * image + src_ref[r, j]
                )
                old_ref[0, j] = current

            operate(u_ref, 0, p, finish)
            field_pair(u_ref, 0, q).start()

        @pl.when(r == STEPS - 1)
        def _():
            def finish(j, image):
                grad = lam_ref[0, j] * image
                for t in range(STEPS - 1):
                    grad = grad + lam_ref[STEPS - 1 - t, j] * img_ref[t, j]
                gp_ref[j, Y:2 * Y, :] = grad

            operate(u_ref, 0, p, finish)

            def pieces(j, carry):
                for k in range(1, NX):
                    xs_ref[k - 1, j] = chunk(j, (px + k) % NX)
                sum_ref[j] = chunk(j, px)
                return carry

            for h in range(2):
                lax.fori_loop(4 * h, 4 * h + 4, pieces, 0)
                for k in (2, 1, 3):
                    reduce_copy(h, k).start()

        prepare(v_ref, 1, p)
        field_pair(v_ref, 1, p).wait_recv()

        @pl.when((r > 0) & (r < STEPS - 1))
        def _():
            field_pair(v_ref, 1, q).wait_send()

        def finish_adjoint(j, image):
            present = lam_ref[r, j]
            earlier = 2.0 * present - old_ref[1, j] + image + inj_ref[STEPS - 1 - r, j]
            old_ref[1, j] = present
            lam_ref[r + 1, j] = earlier
            v_ref[q, X + j, PAD:PAD + Y, :] = cw_ref[j] * earlier

        @pl.when(r == STEPS - 1)
        def _():
            field_pair(v_ref, 1, q).wait_send()

        operate(v_ref, 1, p, finish_adjoint)

        @pl.when(r < STEPS - 1)
        def _():
            field_pair(u_ref, 0, q).wait_send()
            field_pair(v_ref, 1, q).start()

        return carry

    first_forward.wait_send()
    lax.fori_loop(0, STEPS, round_, 0)

    def total_row(j, carry):
        sum_ref[j] = sum_ref[j] + xr_ref[0, j] + xr_ref[1, j] + xr_ref[2, j]
        return carry

    for h in range(2):
        for k in range(1, NX):
            reduce_copy(h, k).wait_recv()
        lax.fori_loop(4 * h, 4 * h + 4, total_row, 0)
        for k in range(1, NZL):
            spread_copy(h, k).start()

    def out_row(j, carry):
        one_ref[0, j] = lam_ref[STEPS - 1, j]
        zero_ref[0, j] = lam_ref[STEPS, j]
        return carry

    lax.fori_loop(0, X, out_row, 0)
    for h in range(2):
        for k in range(1, NZL):
            spread_copy(h, k).wait_recv()
    mine = pl.ds(pl.multiple_of(pz * 8, 8), 8)
    grad_ref[...] = sum_ref[:, mine, :] + zr_ref[0] + zr_ref[1] + zr_ref[2]

    for i in range(fields):
        for k in range(1, NZL):
            z_copy(i, k).wait_send()

    @pl.when(jnp.logical_not(seam))
    def _():
        for i in range(3):
            for k in range(1, NX):
                x_copy(i, k).wait_send()

    for k in range(1, NX):
        x_copy(3, k).wait_send()
    for i in range(3):
        model_pair(i).wait_send()
    field_pair(v_ref, 1, 1).wait_send()
    for h in range(2):
        for k in range(1, NX):
            reduce_copy(h, k).wait_send()
        for k in range(1, NZL):
            spread_copy(h, k).wait_send()


def on_device(
    blocks,
    state_before, state_now, adjoint_later, adjoint_now,
    courant_sq, epsilon, tilt_angle, azimuth,
    aperture_anchor, step_index, wavelet, residual_traces,
    source_x, source_y, source_z, receiver_x, receiver_y, receiver_z,
):
    vmem = pl.BlockSpec(memory_space=pltpu.VMEM)
    smem = pl.BlockSpec(memory_space=pltpu.SMEM)
    v = lambda *shape: pltpu.VMEM(shape, F32)
    dma = lambda *shape: pltpu.SemaphoreType.DMA(shape)
    results = pl.pallas_call(
        functools.partial(kernel, blocks),
        out_shape=(
            pltpu.VMEM((1, X, Y, Z), F32),
            pltpu.VMEM((1, X, Y, Z), F32),
            pltpu.VMEM((X, 8, Z), F32),
        ),
        in_specs=[smem] * 5 + [vmem] * 14,
        out_specs=(vmem, vmem, vmem),
        scratch_shapes=[
            v(4, X, 128, Z), v(3, 2 * X, Y, Z),
            v(2, 3 * X, Y + 2 * PAD, Z), v(2, 3 * X, Y + 2 * PAD, Z),
            v(2, X, Y, Z), v(STEPS + 1, X, Y, Z), v(STEPS - 1, X, Y, Z), v(X, Y, Z),
            v(2 * X, Y, Z), v(2 * X, Y, Z), v(2 * X, Y, Z), v(2 * X, Y, Z), v(2 * X, Y, Z),
            v(2, 2 * X, Y, Z), v(2, X, Y, Z), v(2 * X, Y, Z), v(X, Y + 2 * PAD, Z), v(X, Y, Z),
            v(STEPS - 1, X, Y, Z), v(STEPS, X, Y, Z), v(X, Y, Z),
            v(X, 3 * Y, Z), v(3, X, 32, Z), v(3, X, 32, Z), v(X, 32, Z), v(3, X, 8, Z),
            pltpu.SemaphoreType.REGULAR, dma(4, 3), dma(4, 3), dma(4, 3), dma(4, 3), dma(3, 2), dma(3, 2),
            dma(2, 2, 2), dma(2, 2, 2), dma(2, 3), dma(2, 3), dma(2, 3), dma(2, 3),
        ],
        compiler_params=pltpu.CompilerParams(
            collective_id=0, has_side_effects=True, vmem_limit_bytes=60000 * 1024,
        ),
    )(
        aperture_anchor, step_index, source_x, source_y, source_z,
        wavelet, residual_traces, receiver_x, receiver_y, receiver_z,
        state_before, state_now, adjoint_later, adjoint_now,
        epsilon, tilt_angle, azimuth, courant_sq, depth_matrix(),
    )
    return hand_out([pltpu.with_memory_space_constraint(a, pltpu.VMEM) for a in results])


def hand_out_kernel(*refs):
    sources, targets, sem = refs[:3], refs[3:6], refs[6]
    copies = [pltpu.make_async_copy(a, b, sem.at[n]) for n, (a, b) in enumerate(zip(sources, targets))]
    for copy in copies:
        copy.start()
    for copy in copies:
        copy.wait()


def hand_out(arrays):
    return pl.pallas_call(
        hand_out_kernel,
        out_shape=tuple(jax.ShapeDtypeStruct(a.shape, a.dtype) for a in arrays),
        in_specs=[pl.BlockSpec(memory_space=pltpu.VMEM)] * 3,
        out_specs=(pl.BlockSpec(memory_space=pl.ANY),) * 3,
        scratch_shapes=[pltpu.SemaphoreType.DMA((3,))],
    )(*arrays)


def solution(mesh):
    field = P("shot", "blk", None, None)
    model = P("blk", "shot", None)
    in_specs = (
        (field,) * 4 + (model,) * 4
        + (P("shot"), P(), P("shot", None), P("shot", None, None))
        + (P("shot"),) * 3 + (P("shot", None),) * 3
    )
    return jax.shard_map(
        functools.partial(on_device, mesh.shape["blk"]),
        mesh=mesh, in_specs=in_specs, out_specs=(field, field, model), check_vma=False,
    )
```

```python
import functools
import math

import numpy as np
import jax
import jax.numpy as jnp
from jax import lax
from jax.experimental import pallas as pl
from jax.experimental.pallas import tpu as pltpu
from jax.sharding import PartitionSpec as P

STEPS = 4
COEF = (0.8, -0.2, 4.0 / 105.0, -1.0 / 280.0)
WHOLE = (672, -168, 32, -3)
MESH = pl.DeviceIdType.MESH
F32 = jnp.float32

X, Y, Z = 8, 64, 128
PAD = 8
PLACES = 9
NX, NZL = 4, 4


def depth_matrix():
    m = np.zeros((Z, Z), np.float32)
    for k in range(1, 5):
        for j in range(Z):
            if j + k < Z:
                m[j + k, j] += WHOLE[k - 1]
            if j - k >= 0:
                m[j - k, j] -= WHOLE[k - 1]
    return jnp.asarray(np.concatenate([m, m], 0), jnp.bfloat16)


def sin_cos(angle):
    square = angle * angle
    sine = jnp.full_like(angle, 1.0 / math.factorial(13))
    for n in (11, 9, 7, 5, 3, 1):
        sine = sine * square + (-1.0) ** (n // 2) / math.factorial(n)
    cosine = jnp.full_like(angle, -1.0 / math.factorial(14))
    for n in (12, 10, 8, 6, 4, 2, 0):
        cosine = cosine * square + (-1.0) ** (n // 2) / math.factorial(n)
    return sine * angle, cosine


def depth_diff(flat, matrix):
    upper = flat.astype(jnp.bfloat16)
    lower = (flat - upper.astype(F32)).astype(jnp.bfloat16)
    both = jnp.concatenate([upper, lower], axis=1)
    return jnp.dot(both, matrix, preferred_element_type=F32) * (1.0 / 840.0)


def kernel(
    blocks,
    anchor_ref, step_ref, sx_ref, sy_ref, sz_ref,
    wave_ref, residual_ref, rx_ref, ry_ref, rz_ref,
    before_ref, now_ref, later_ref, adj_ref,
    eps_ref, tilt_ref, az_ref, c_ref, mat_ref,
    one_ref, zero_ref, grad_ref,
    g_ref, m_ref, u_ref, v_ref, old_ref, lam_ref, img_ref, cw_ref,
    e1_ref, e_ref, nx_ref, ny_ref, nz_ref,
    slz_ref, sly_ref, fx_ref, fy_ref, fz_ref, src_ref, inj_ref, plane_ref,
    gp_ref, xs_ref, xr_ref, sum_ref, zr_ref,
    go_sem, zs_sem, zr_sem, xs_sem, xr_sem, ms_sem, mr_sem,
    fs_sem, fr_sem, rs_sem, rr_sem, qs_sem, qr_sem,
):
    shot = lax.axis_index("shot")
    blk = lax.axis_index("blk")
    px = shot // NZL
    pz = shot % NZL
    has_left = blk > 0
    has_right = blk < blocks - 1
    seam = (blk == blocks // 2 - 1) | (blk == blocks // 2)
    mate = (blk == blocks // 2 - 2) | (blk == blocks // 2 + 1)
    shots_z = [px * NZL + (pz + k) % NZL for k in range(1, NZL)]
    shots_x = [((px + k) % NX) * NZL + pz for k in range(1, NX)]

    barrier = pltpu.get_barrier_semaphore()
    for other in shots_z + shots_x:
        pl.semaphore_signal(barrier, inc=1, device_id=(other, blk), device_id_type=MESH)

    @pl.when(has_left)
    def _():
        pl.semaphore_signal(barrier, inc=1, device_id=(shot, blk - 1), device_id_type=MESH)

    @pl.when(has_right)
    def _():
        pl.semaphore_signal(barrier, inc=1, device_id=(shot, blk + 1), device_id_type=MESH)

    peers = len(shots_z) + len(shots_x)

    @pl.when(has_left & has_right)
    def _():
        pl.semaphore_wait(barrier, peers + 2)

    @pl.when(jnp.logical_not(has_left & has_right))
    def _():
        pl.semaphore_wait(barrier, peers + 1)

    def remote(src, dst, ssem, rsem, device):
        return pltpu.make_async_remote_copy(
            src_ref=src, dst_ref=dst, send_sem=ssem, recv_sem=rsem,
            device_id=device, device_id_type=MESH,
        )

    class Pair:
        def __init__(self, src_right, dst_left_halo, src_left, dst_right_halo, ssem, rsem):
            self.right = remote(src_right, dst_left_halo, ssem.at[0], rsem.at[0], (shot, blk + 1))
            self.left = remote(src_left, dst_right_halo, ssem.at[1], rsem.at[1], (shot, blk - 1))

        def start(self):
            @pl.when(has_right)
            def _():
                self.right.start()

            @pl.when(has_left)
            def _():
                self.left.start()

        def wait_recv(self):
            @pl.when(has_left)
            def _():
                self.right.wait_recv()

            @pl.when(has_right)
            def _():
                self.left.wait_recv()

        def wait_send(self):
            @pl.when(has_right)
            def _():
                self.right.wait_send()

            @pl.when(has_left)
            def _():
                self.left.wait_send()

    def field_pair(ref, chain, p, src=None):
        own = ref.at[p, X:2 * X, PAD:PAD + Y] if src is None else src
        return Pair(
            own, ref.at[p, 0:X, PAD:PAD + Y], own, ref.at[p, 2 * X:3 * X, PAD:PAD + Y],
            fs_sem.at[chain, p], fr_sem.at[chain, p],
        )

    models = (eps_ref, tilt_ref, az_ref, c_ref)
    fields = len(models)

    def z_copy(i, k):
        rows = pl.ds(pl.multiple_of(shot * 8, 8), 8)
        return remote(models[i], g_ref.at[i, :, rows], zs_sem.at[i, k - 1], zr_sem.at[i, k - 1], (shots_z[k - 1], blk))

    def x_copy(i, k):
        rows = pl.ds(pl.multiple_of(px * 32, 8), 32)
        part = g_ref.at[i, :, rows]
        return remote(part, part, xs_sem.at[i, k - 1], xr_sem.at[i, k - 1], (shots_x[k - 1], blk))

    for i in range(fields):
        for k in range(1, NZL):
            z_copy(i, k).start()
    first_forward = field_pair(u_ref, 0, 0, now_ref.at[0])

    own_rows = pl.ds(pl.multiple_of(shot * 8, 8), 8)
    for i in range(fields):
        g_ref[i, :, own_rows, :] = models[i][...]
    zeros_y = jnp.zeros((3 * X, PAD, Z), F32)
    for p in range(2):
        for ref in (u_ref, v_ref):
            ref[p, :, 0:PAD, :] = zeros_y
            ref[p, :, PAD + Y:, :] = zeros_y
    fy_ref[:, 0:PAD, :] = jnp.zeros((X, PAD, Z), F32)
    fy_ref[:, PAD + Y:, :] = jnp.zeros((X, PAD, Z), F32)

    def edge(at, m_at):
        def row(j, carry):
            for p in range(2):
                for ref in (u_ref, v_ref):
                    ref[p, at + j, PAD:PAD + Y, :] = jnp.zeros((Y, Z), F32)
            return carry

        lax.fori_loop(0, X, row, 0)

        def m_row(j, carry):
            for i in range(3):
                m_ref[i, m_at + j] = jnp.zeros((Y, Z), F32)
            return carry

        lax.fori_loop(0, 4, m_row, 0)

    @pl.when(blk == 0)
    def _():
        edge(0, 0)

    @pl.when(blk == blocks - 1)
    def _():
        edge(2 * X, 12)


    step = step_ref[0]
    anchor = jnp.full((Y, Z), anchor_ref[0], jnp.int32)
    row_y = lax.broadcasted_iota(jnp.int32, (Y, Z), 0)
    col_z = lax.broadcasted_iota(jnp.int32, (Y, Z), 1)
    at_yz = (row_y == sy_ref[0]) & (col_z == sz_ref[0])
    local_x = jnp.full((Y, Z), sx_ref[0] - blk * X, jnp.int32)
    times = lax.broadcasted_iota(jnp.int32, (1, 16), 1)
    amplitudes = [
        jnp.sum(jnp.where(times == step + t, wave_ref[...], 0.0), axis=1, keepdims=True)
        for t in range(STEPS - 1)
    ]

    def source_row(j, carry):
        here = at_yz & (local_x == j)
        for t in range(STEPS - 1):
            src_ref[t, j] = jnp.where(here, jnp.broadcast_to(amplitudes[t], (Y, Z)), 0.0)
        return carry

    def setup_row(j, carry):
        u_ref[0, X + j, PAD:PAD + Y, :] = now_ref[0, j]
        old_ref[0, j] = before_ref[0, j]
        old_ref[1, j] = later_ref[0, j]
        lam_ref[0, j] = adj_ref[0, j]
        gp_ref[j] = jnp.zeros((3 * Y, Z), F32)
        return carry

    lax.fori_loop(0, X, setup_row, 0)

    for i in range(fields):
        for k in range(1, NZL):
            z_copy(i, k).wait_recv()
        if i == 0:
            @pl.when(mate)
            def _():
                pl.semaphore_wait(go_sem, 1)

        for k in (2, 1, 3):
            x_copy(i, k).start()
        if i == 1:
            first_forward.start()
    first_adjoint = field_pair(v_ref, 1, 0)

    local_r = rx_ref[...] - blk * X

    def plane_row(j, carry):
        hit = (jnp.broadcast_to(ry_ref[...], (Y, Z)) == row_y) & (jnp.broadcast_to(local_r, (Y, Z)) == j)
        plane_ref[j] = jnp.where(hit, 1.0, 0.0)
        return carry

    sample_row = lax.broadcasted_iota(jnp.int32, (16, Z), 0)
    depth_row = lax.broadcasted_iota(jnp.int32, (Z, Z), 0)
    at_depth = jnp.broadcast_to(rz_ref[...], (Z, Z)) == depth_row

    def inject(t, carry):
        samples = jnp.sum(jnp.where(sample_row == step + t, residual_ref[0], 0.0), axis=0, keepdims=True)
        rest = jnp.where(at_depth, jnp.broadcast_to(samples, (Z, Z)), 0.0)
        parts = []
        for _ in range(3):
            part = rest.astype(jnp.bfloat16)
            parts.append(part)
            rest = rest - part.astype(F32)
        depths = jnp.concatenate(parts, axis=1)
        for h in range(2):
            planes = plane_ref[4 * h:4 * h + 4].reshape(4 * Y, Z).astype(jnp.bfloat16)
            total = lax.dot_general(
                jnp.concatenate([planes] * 3, axis=1), depths, (((1,), (1,)), ((), ())),
                preferred_element_type=F32,
            )
            inj_ref[t, 4 * h:4 * h + 4] = total.reshape(4, Y, Z)
        return carry

    def set_sources():
        lax.fori_loop(0, X, source_row, 0)
        lax.fori_loop(0, X, plane_row, 0)
        lax.fori_loop(0, STEPS, inject, 0)

    @pl.when(seam)
    def _():
        for i in range(3):
            for k in range(1, NX):
                x_copy(i, k).wait_send()
        pl.semaphore_signal(go_sem, inc=1, device_id=(shot, blk + 1 - 2 * (blk % 2)), device_id_type=MESH)

    @pl.when(jnp.logical_not(seam))
    def _():
        set_sources()

    def model_pair(i):
        m = m_ref.at[i]
        return Pair(m.at[8:12], m.at[0:4], m.at[4:8], m.at[12:16], ms_sem.at[i], mr_sem.at[i])

    def picked(load, where):
        total = load(0)
        for a in range(1, PLACES):
            total = jnp.where(where == 8 * a, load(a), total)
        return total

    def take(i):
        for k in (1, 3, 2):
            x_copy(i, k).wait_recv()

        def row(j, carry):
            window = picked(lambda a: g_ref[i, j, 8 * a:8 * a + Y, :], anchor)
            if i == 3:
                cw_ref[j] = window
                v_ref[0, X + j, PAD:PAD + Y, :] = window * adj_ref[0, j]
            else:
                m_ref[i, 4 + j] = window
            return carry

        lax.fori_loop(0, X, row, 0)
        if i == 3:
            first_adjoint.start()
        else:
            model_pair(i).start()

    def tilt_row(i, carry):
        level, upright = sin_cos(m_ref[1, i])
        nx_ref[i] = level
        nz_ref[i] = upright
        return carry

    def tensor_row(i, carry):
        outside = ((blk == 0) & (i < 4)) | ((blk == blocks - 1) & (i >= 12))
        twice = 2.0 * m_ref[0, i]
        turn = m_ref[2, i]
        level = nx_ref[i]
        half_sin, half_cos = sin_cos(0.5 * turn)
        e_ref[i] = twice
        e1_ref[i] = jnp.where(outside, 0.0, 1.0 + twice)
        nx_ref[i] = level * (1.0 - 2.0 * half_sin * half_sin)
        ny_ref[i] = level * (2.0 * half_sin * half_cos)
        return carry

    for i in range(3):
        take(i)
    lax.fori_loop(4, 12, tilt_row, 0)
    lax.fori_loop(4, 12, tensor_row, 0)
    take(3)

    @pl.when(seam)
    def _():
        set_sources()


    matrix = mat_ref[...]

    def x_diff(ref, at):
        total = None
        for k in range(1, 5):
            term = COEF[k - 1] * (ref[at + k] - ref[at - k])
            total = term if total is None else total + term
        return total

    def slope_z(field, n, h):
        flat = field[pl.ds(4 + 4 * h, 4), PAD:PAD + Y, :].reshape(4 * Y, Z)
        slz_ref[n, pl.ds(4 * h, 4)] = depth_diff(flat, matrix).reshape(4, Y, Z)

    def slope_y(field, i):
        total = None
        for k in range(1, 5):
            term = COEF[k - 1] * (field[i, PAD + k:PAD + k + Y, :] - field[i, PAD - k:PAD - k + Y, :])
            total = term if total is None else total + term
        return total

    def prepare(ref, n, p):
        field = ref.at[p]
        slope_z(field, n, 1)
        slope_z(field, n, 2)

        def row(j, carry):
            sly_ref[n, j] = slope_y(field, X + j)
            return carry

        lax.fori_loop(0, X, row, 0)

    def operate(ref, n, p, finish):
        field = ref.at[p]
        slope_z(field, n, 0)
        slope_z(field, n, 3)

        def fluxes(i, own):
            slx = None
            for k in range(1, 5):
                tx = COEF[k - 1] * (field[i + 4 + k, PAD:PAD + Y, :] - field[i + 4 - k, PAD:PAD + Y, :])
                slx = tx if slx is None else slx + tx
            sly = sly_ref[n, i - 4] if own else slope_y(field, i + 4)
            slz = slz_ref[n, i]
            nx, ny, nz = nx_ref[i], ny_ref[i], nz_ref[i]
            pull = e_ref[i] * (nx * slx + ny * sly + nz * slz)
            e1 = e1_ref[i]
            fx_ref[i] = e1 * slx - nx * pull
            if own:
                fy_ref[i - 4, PAD:PAD + Y, :] = e1 * sly - ny * pull
                fz_ref[i - 4] = e1 * slz - nz * pull

        def halo_row(i, carry):
            fluxes(i, False)
            fluxes(i + 12, False)
            return carry

        def own_row(i, carry):
            fluxes(i + 4, True)
            return carry

        lax.fori_loop(0, 4, halo_row, 0)
        lax.fori_loop(0, X, own_row, 0)

        def flux_z(h, carry):
            flat = fz_ref[pl.ds(4 * h, 4)].reshape(4 * Y, Z)
            fz_ref[pl.ds(4 * h, 4)] = depth_diff(flat, matrix).reshape(4, Y, Z)
            return carry

        lax.fori_loop(0, 2, flux_z, 0)

        def result_row(j, carry):
            total = x_diff(fx_ref, j + 4)
            for k in range(1, 5):
                total = total + COEF[k - 1] * (
                    fy_ref[j, PAD + k:PAD + k + Y, :] - fy_ref[j, PAD - k:PAD - k + Y, :]
                )
            finish(j, total + fz_ref[j])
            return carry

        lax.fori_loop(0, X, result_row, 0)

    def reduce_copy(h, k):
        half = pl.ds(4 * h, 4)
        return remote(
            xs_ref.at[k - 1, half], xr_ref.at[k - 1, half], rs_sem.at[h, k - 1], rr_sem.at[h, k - 1],
            (shots_x[k - 1], blk),
        )

    def spread_copy(h, k):
        half = pl.ds(4 * h, 4)
        rows = pl.ds(pl.multiple_of(((pz + k) % NZL) * 8, 8), 8)
        return remote(
            sum_ref.at[half, rows], zr_ref.at[k - 1, half], qs_sem.at[h, k - 1], qr_sem.at[h, k - 1],
            (shots_z[k - 1], blk),
        )

    anchor_part = jnp.full((32, Z), anchor_ref[0], jnp.int32)

    def chunk(j, target):
        return picked(
            lambda a: gp_ref[j, pl.ds(pl.multiple_of(Y + 32 * target - 8 * a, 8), 32), :], anchor_part
        )

    def round_(r, carry):
        p = lax.rem(r, 2)
        q = 1 - p
        coming = field_pair(u_ref, 0, p)
        @pl.when(r > 0)
        def _():
            prepare(u_ref, 0, p)

        coming.wait_recv()

        @pl.when(r < STEPS - 1)
        def _():
            def finish(j, image):
                img_ref[r, j] = image
                current = u_ref[p, X + j, PAD:PAD + Y, :]
                u_ref[q, X + j, PAD:PAD + Y, :] = (
                    2.0 * current - old_ref[0, j] + cw_ref[j] * image + src_ref[r, j]
                )
                old_ref[0, j] = current

            operate(u_ref, 0, p, finish)
            field_pair(u_ref, 0, q).start()

        @pl.when(r == STEPS - 1)
        def _():
            def finish(j, image):
                grad = lam_ref[0, j] * image
                for t in range(STEPS - 1):
                    grad = grad + lam_ref[STEPS - 1 - t, j] * img_ref[t, j]
                gp_ref[j, Y:2 * Y, :] = grad

            operate(u_ref, 0, p, finish)

            def pieces(j, carry):
                for k in range(1, NX):
                    xs_ref[k - 1, j] = chunk(j, (px + k) % NX)
                sum_ref[j] = chunk(j, px)
                return carry

            for h in range(2):
                lax.fori_loop(4 * h, 4 * h + 4, pieces, 0)
                for k in (2, 1, 3):
                    reduce_copy(h, k).start()

        @pl.when(r > 0)
        def _():
            prepare(v_ref, 1, p)

        field_pair(v_ref, 1, p).wait_recv()

        @pl.when((r > 0) & (r < STEPS - 1))
        def _():
            field_pair(v_ref, 1, q).wait_send()

        def finish_adjoint(j, image):
            present = lam_ref[r, j]
            earlier = 2.0 * present - old_ref[1, j] + image + inj_ref[STEPS - 1 - r, j]
            old_ref[1, j] = present
            lam_ref[r + 1, j] = earlier
            v_ref[q, X + j, PAD:PAD + Y, :] = cw_ref[j] * earlier

        @pl.when(r == STEPS - 1)
        def _():
            field_pair(v_ref, 1, q).wait_send()

        operate(v_ref, 1, p, finish_adjoint)

        @pl.when(r < STEPS - 1)
        def _():
            field_pair(u_ref, 0, q).wait_send()
            field_pair(v_ref, 1, q).start()

        return carry

    prepare(u_ref, 0, 0)
    prepare(v_ref, 1, 0)
    for i in range(2):
        model_pair(i).wait_recv()

    def tilt_halo(i, carry):
        tilt_row(i, carry)
        return tilt_row(i + 12, carry)

    lax.fori_loop(0, 4, tilt_halo, 0)
    model_pair(2).wait_recv()

    def tensor_halo(i, carry):
        tensor_row(i, carry)
        return tensor_row(i + 12, carry)

    lax.fori_loop(0, 4, tensor_halo, 0)
    first_forward.wait_send()
    lax.fori_loop(0, STEPS, round_, 0)

    def total_row(j, carry):
        sum_ref[j] = sum_ref[j] + xr_ref[0, j] + xr_ref[1, j] + xr_ref[2, j]
        return carry

    for h in range(2):
        for k in range(1, NX):
            reduce_copy(h, k).wait_recv()
        lax.fori_loop(4 * h, 4 * h + 4, total_row, 0)
        for k in range(1, NZL):
            spread_copy(h, k).start()

    def out_row(j, carry):
        one_ref[0, j] = lam_ref[STEPS - 1, j]
        zero_ref[0, j] = lam_ref[STEPS, j]
        return carry

    lax.fori_loop(0, X, out_row, 0)
    for h in range(2):
        for k in range(1, NZL):
            spread_copy(h, k).wait_recv()
    mine = pl.ds(pl.multiple_of(pz * 8, 8), 8)
    grad_ref[...] = sum_ref[:, mine, :] + zr_ref[0] + zr_ref[1] + zr_ref[2]

    for i in range(fields):
        for k in range(1, NZL):
            z_copy(i, k).wait_send()

    @pl.when(jnp.logical_not(seam))
    def _():
        for i in range(3):
            for k in range(1, NX):
                x_copy(i, k).wait_send()

    for k in range(1, NX):
        x_copy(3, k).wait_send()
    for i in range(3):
        model_pair(i).wait_send()
    field_pair(v_ref, 1, 1).wait_send()
    for h in range(2):
        for k in range(1, NX):
            reduce_copy(h, k).wait_send()
        for k in range(1, NZL):
            spread_copy(h, k).wait_send()


def on_device(
    blocks,
    state_before, state_now, adjoint_later, adjoint_now,
    courant_sq, epsilon, tilt_angle, azimuth,
    aperture_anchor, step_index, wavelet, residual_traces,
    source_x, source_y, source_z, receiver_x, receiver_y, receiver_z,
):
    vmem = pl.BlockSpec(memory_space=pltpu.VMEM)
    smem = pl.BlockSpec(memory_space=pltpu.SMEM)
    v = lambda *shape: pltpu.VMEM(shape, F32)
    dma = lambda *shape: pltpu.SemaphoreType.DMA(shape)
    results = pl.pallas_call(
        functools.partial(kernel, blocks),
        out_shape=(
            pltpu.VMEM((1, X, Y, Z), F32),
            pltpu.VMEM((1, X, Y, Z), F32),
            pltpu.VMEM((X, 8, Z), F32),
        ),
        in_specs=[smem] * 5 + [vmem] * 14,
        out_specs=(vmem, vmem, vmem),
        scratch_shapes=[
            v(4, X, 128, Z), v(3, 2 * X, Y, Z),
            v(2, 3 * X, Y + 2 * PAD, Z), v(2, 3 * X, Y + 2 * PAD, Z),
            v(2, X, Y, Z), v(STEPS + 1, X, Y, Z), v(STEPS - 1, X, Y, Z), v(X, Y, Z),
            v(2 * X, Y, Z), v(2 * X, Y, Z), v(2 * X, Y, Z), v(2 * X, Y, Z), v(2 * X, Y, Z),
            v(2, 2 * X, Y, Z), v(2, X, Y, Z), v(2 * X, Y, Z), v(X, Y + 2 * PAD, Z), v(X, Y, Z),
            v(STEPS - 1, X, Y, Z), v(STEPS, X, Y, Z), v(X, Y, Z),
            v(X, 3 * Y, Z), v(3, X, 32, Z), v(3, X, 32, Z), v(X, 32, Z), v(3, X, 8, Z),
            pltpu.SemaphoreType.REGULAR, dma(4, 3), dma(4, 3), dma(4, 3), dma(4, 3), dma(3, 2), dma(3, 2),
            dma(2, 2, 2), dma(2, 2, 2), dma(2, 3), dma(2, 3), dma(2, 3), dma(2, 3),
        ],
        compiler_params=pltpu.CompilerParams(
            collective_id=0, has_side_effects=True, vmem_limit_bytes=60000 * 1024,
        ),
    )(
        aperture_anchor, step_index, source_x, source_y, source_z,
        wavelet, residual_traces, receiver_x, receiver_y, receiver_z,
        state_before, state_now, adjoint_later, adjoint_now,
        epsilon, tilt_angle, azimuth, courant_sq, depth_matrix(),
    )
    return hand_out([pltpu.with_memory_space_constraint(a, pltpu.VMEM) for a in results])


def hand_out_kernel(*refs):
    sources, targets, sem = refs[:3], refs[3:6], refs[6]
    copies = [pltpu.make_async_copy(a, b, sem.at[n]) for n, (a, b) in enumerate(zip(sources, targets))]
    for copy in copies:
        copy.start()
    for copy in copies:
        copy.wait()


def hand_out(arrays):
    return pl.pallas_call(
        hand_out_kernel,
        out_shape=tuple(jax.ShapeDtypeStruct(a.shape, a.dtype) for a in arrays),
        in_specs=[pl.BlockSpec(memory_space=pltpu.VMEM)] * 3,
        out_specs=(pl.BlockSpec(memory_space=pl.ANY),) * 3,
        scratch_shapes=[pltpu.SemaphoreType.DMA((3,))],
    )(*arrays)


def solution(mesh):
    field = P("shot", "blk", None, None)
    model = P("blk", "shot", None)
    in_specs = (
        (field,) * 4 + (model,) * 4
        + (P("shot"), P(), P("shot", None), P("shot", None, None))
        + (P("shot"),) * 3 + (P("shot", None),) * 3
    )
    return jax.shard_map(
        functools.partial(on_device, mesh.shape["blk"]),
        mesh=mesh, in_specs=in_specs, out_specs=(field, field, model), check_vma=False,
    )
```
